128 devices in a mesh: ue: 16 (over z, y), cell: 8 (over x, core).
Axes of the slice: x: 4, y: 4, z: 4, core: 2. Of those that a mesh axis runs over, the one named last changes fastest.
Arguments:
- gains: bfloat16 [2048, 32, 128, 128], P('ue', 'cell'), may hold values from 0 to 2.4414062
- near_blocks: int32 [2048, 32], P('ue', 'cell'), may hold values from 0 to 127, as said below
- serve_block: int32 [262144, 1], P(('ue', 'cell')), may hold values from 0 to 127; in each aligned block of 2048 rows (0 to 2047, 2048 to 4095, ...) at most 48 rows name the same one
- serve_cell: int32 [262144], P(('ue', 'cell')), may hold values from 0 to 127
- serve_gain: float32 [262144], P(('ue', 'cell')), may hold values from 0.2 to 5
- power_init: float32 [32, 16384], P(None, ('ue', 'cell')), may hold values from 0.01 to 2
- avg_init: float32 [262144], P(('ue', 'cell')), may hold values from 0.05 to 1
Outputs:
- avg_out: float32 [262144], P(('ue', 'cell'))
- power_out: float32 [32, 16384], P(None, ('ue', 'cell'))
The draws below stay inside these ranges and needn't reach their ends.
Inputs may be any that keep to these rules, and one draw needn't show every extreme that they name: `near_blocks`: for each UE block, the entries in columns j * 4 to (j + 1) * 4 - 1 are distinct cell blocks, each equal to j modulo 8. `serve_block`: within the 2048 UEs of each aligned block, at most 48 have the same serving cell block, and some cell block serves exactly 48 of them.
All inputs are finite; a program needn't handle non-finite values.
Results may differ from the reference program's by a relative error of at most 0.002.
Values may be sent and summed in bfloat16 or wider, within the bound.
No kernel may reach another device: no remote copies, remote signals or barrier semaphores. Data moves between devices by JAX's collectives and lax.ppermute only.
A program may use at most 128 MiB of HBM per device.

```python
import math
import jax
import jax.numpy as jnp
import numpy as np
from jax import lax

SUBBANDS = 32
BLK = 128
UE_DEV = 2048
NEAR_DEV = 4
SLOTS = 4
GROUPS = 8
UE_GROUPS = 16
CAP = 48
UES = 262144
CELL_BLOCKS = 128
CELLS = 16384
UE_BLOCKS = 2048


def near_table(key):
    scores = jax.random.randint(key, (UE_BLOCKS, GROUPS, UE_GROUPS), 0, 1 << 20)
    scores = scores * UE_GROUPS + jnp.arange(UE_GROUPS, dtype=jnp.int32)[None, None, :]
    order = jnp.argsort(scores, axis=-1)
    picked = order[:, :, :NEAR_DEV].astype(jnp.int32)
    blocks = jnp.arange(GROUPS, dtype=jnp.int32)[None, :, None] + GROUPS * picked
    return blocks.reshape(UE_BLOCKS, GROUPS * NEAR_DEV).astype(jnp.int32)


def cell_log_factor(key):
    return jax.random.uniform(jax.random.fold_in(key, 31), (CELLS,), jnp.float32, -2.5, 2.5)


def draw_near_blocks(key, part):
    return near_table(key)


def draw_gains(key, part):
    shape = (UE_BLOCKS, NEAR_DEV * GROUPS, BLK, BLK)
    terms_total = NEAR_DEV * GROUPS * BLK
    near = near_table(key)
    log_factor = cell_log_factor(key).reshape(CELL_BLOCKS, BLK)
    factor = jnp.exp(log_factor[near])[:, :, :, None]
    level = jnp.clip(jax.random.normal(jax.random.fold_in(key, 11), shape, jnp.float32), -4.0, 4.0)
    values = 4.0 / terms_total * factor * jnp.exp(1.2 * level) / 5.0
    return values.astype(jnp.float32).astype(jnp.bfloat16)


def draw_power_init(key, part):
    log_factor = cell_log_factor(key)[None, :]
    noise = jax.random.uniform(jax.random.fold_in(key, 41), (SUBBANDS, CELLS), jnp.float32, 0.0, 1.0)
    mixed = 0.7 * (2.5 - log_factor) / 5.0 + 0.3 * noise
    mixed = jnp.clip(mixed, 0.0, 1.0)
    return (0.01 * jnp.exp(5.298317 * mixed)).astype(jnp.float32)


def place_ends(result, own_key, smallest, largest):
    longest = result.shape.index(max(result.shape))
    spots = []
    for shift in (0, 1):
        where = [jax.random.randint(jax.random.fold_in(own_key, axis), (), 0, length) for axis, length in enumerate(result.shape)]
        where[longest] = (where[longest] + shift) % result.shape[longest]
        spots.append(tuple(where))
    return result.at[spots[0]].set(smallest).at[spots[1]].set(largest)


def block_scale(rng, extent, split, least, largest):
    def one(dim, parts):
        draws = jax.random.uniform(jax.random.fold_in(jax.random.fold_in(rng, 6), dim), (parts,), jnp.float32, least / len(split), largest / len(split))
        return jnp.repeat(jnp.exp(draws), extent[dim] // parts).reshape((-1,) + (1,) * (len(extent) - dim - 1))

    gain = one(*split[0])
    for cut in split[1:]:
        gain = gain * one(*cut)
    return gain


def routed_block(stream_key, own, number, rows, count, top, reach, slope):
    ranking = jax.random.permutation(stream_key, count)
    crowded, common = portions_of(count, rows * top, reach, slope, True), portions_of(count, rows * top, reach, slope, False)
    places = jnp.arange(count)

    def named(lengths, rotation):
        used = int((lengths > 0).sum())
        fixed = max(1, used // 4)
        moved = fixed + (places - fixed + rotation * (used - fixed)) % max(1, count - fixed)
        return jnp.zeros((count,), jnp.int32).at[ranking[jnp.where(places < fixed, places, moved)]].set(jnp.asarray(lengths, jnp.int32))

    lengths = jnp.where(number % 4 == 0, named(crowded, number // 4), named(common, number - number // 4 - 1))
    mixed = jax.random.permutation(jax.random.fold_in(own, 3), count)
    giver, sink = mixed[0:count // 2 * 2:2], mixed[1:count // 2 * 2:2]
    room = jnp.minimum(lengths[giver] - 1, reach - lengths[sink]) // 2
    room = jnp.where((giver == ranking[0]) | (sink == ranking[0]) | (lengths[sink] == 0), 0, jnp.maximum(room, 0))
    moved = jax.random.randint(jax.random.fold_in(own, 4), (count // 2,), 0, 1 << 20) % (room + 1)
    lengths = lengths.at[giver].add(-moved).at[sink].add(moved)
    members = jnp.searchsorted(jnp.cumsum(lengths), jnp.arange(rows * top), side="right").astype(jnp.int32)
    listing = members.reshape(top, rows).T
    listing = listing[jax.random.permutation(jax.random.fold_in(own, 1), rows)]
    rotation = jax.random.randint(jax.random.fold_in(own, 2), (rows, 1), 0, top)
    return jnp.take_along_axis(listing, (jnp.arange(top)[None, :] + rotation) % top, axis=1)


def portions_of(number_of, total, most, lean, full):
    loads = [(1 << 20) // math.isqrt(grade ** lean) + 1 for grade in range(1, number_of + 1)]
    largest = most if full else min(most, max(-(-total // number_of), total * loads[0] // sum(loads)))
    least = 1 if total - largest >= number_of - 1 else 0
    given, surplus = [largest] + [least] * (number_of - 1), total - largest - least * (number_of - 1)
    while surplus > 0:
        candidates = [i for i in range(1, number_of) if given[i] < largest] or [i for i in range(1, number_of) if given[i] < most]
        whole, remaining = sum([loads[i] for i in candidates]), surplus
        for i in candidates:
            more = min(most - given[i], max(1, remaining * loads[i] // whole), surplus)
            given[i] = given[i] + more
            surplus = surplus - more
    return np.array(given)


def setup_inputs(seed: int = 0) -> dict:
    splits = jax.random.split(jax.random.key(seed), 8)
    gains = draw_gains(jax.random.fold_in(splits[7], 71), 0)
    near_blocks = draw_near_blocks(jax.random.fold_in(splits[7], 71), 0)
    serve_block_keys = jax.random.split(jax.random.fold_in(splits[2], 1), UES // UE_DEV)
    serve_block_turns = jax.random.permutation(jax.random.fold_in(splits[2], 3), UES // UE_DEV)
    serve_block = jax.vmap(lambda own, number: routed_block(jax.random.fold_in(splits[2], 2), own, number, UE_DEV, CELL_BLOCKS, 1, CAP, 2))(serve_block_keys, serve_block_turns).reshape((UES, 1))
    serve_cell = place_ends(jax.random.randint(splits[3], (UES,), 0, BLK), jax.random.fold_in(splits[3], 1), 0, BLK - 1).astype(jnp.int32)
    serve_gain = jnp.clip(jnp.exp(math.log(5.0) - 3.218876 * jax.random.uniform(splits[4], (UES,), jnp.float32) ** block_scale(splits[4], (UES,), ((0, 128),), -0.2, 0.2)), 0.2, 5.0)
    power_init = draw_power_init(jax.random.fold_in(splits[7], 71), 0)
    avg_init = jnp.clip(jnp.exp(math.log(1.0) - 2.9957323 * jax.random.uniform(splits[6], (UES,), jnp.float32) ** block_scale(splits[6], (UES,), ((0, 128),), -0.2, 0.2)), 0.05, 1.0)
    return {"gains": gains, "near_blocks": near_blocks, "serve_block": serve_block, "serve_cell": serve_cell, "serve_gain": serve_gain, "power_init": power_init, "avg_init": avg_init}


NOISE_FLOOR = 0.5
KEEP_RATE = 0.7
NEW_RATE = 0.3


def block_terms(power_table, gains, near_blocks):
    group_size = 8
    weight_groups = gains.reshape(UE_BLOCKS // group_size, group_size, NEAR_DEV * GROUPS, BLK, BLK)
    index_groups = near_blocks.reshape(UE_BLOCKS // group_size, group_size, NEAR_DEV * GROUPS)

    def one_group(pair):
        weight_piece, index_piece = pair
        chosen = power_table[index_piece]
        return jnp.einsum("bksw,bkwv->bsv", chosen.astype(jnp.float32), weight_piece.astype(jnp.float32))

    summed = lax.map(one_group, (weight_groups, index_groups))
    summed = summed.reshape(UE_BLOCKS, SUBBANDS, BLK)
    return summed.transpose(1, 0, 2).reshape(SUBBANDS, UES)


def reference(gains, near_blocks, serve_block, serve_cell, serve_gain, power_init, avg_init):
    cell_index = (serve_block[:, 0] * BLK + serve_cell).astype(jnp.int32)
    power_state = power_init
    average = avg_init
    for turn_index in range(SLOTS):
        low_power = power_state.astype(jnp.bfloat16)
        power_table = low_power.reshape(SUBBANDS, CELL_BLOCKS, BLK).transpose(1, 0, 2)
        levels = block_terms(power_table, gains, near_blocks)
        signal = serve_gain[None, :] * power_state[:, cell_index]
        log_rate = jnp.log1p(signal / (levels + NOISE_FLOOR))
        metric = log_rate / average[None, :]
        cell_load = jax.ops.segment_sum(metric.T, cell_index, num_segments=CELLS).T
        shares = metric / cell_load[:, cell_index]
        average = KEEP_RATE * average + NEW_RATE * jnp.sum(shares * log_rate, axis=0)
        demand = 1.0 + cell_load
        power_state = 0.5 * power_state + 0.5 * SUBBANDS * demand / jnp.sum(demand, axis=0, keepdims=True)
    return average, power_state
```

```python
import functools
import jax
import jax.numpy as jnp
from jax import lax
from jax.experimental import pallas as pl
from jax.experimental.pallas import tpu as pltpu
from jax.sharding import Mesh, PartitionSpec as P

SLOTS = 4
NOISE_FLOOR = 0.5
KEEP_RATE = 0.7
NEW_RATE = 0.3
SUB = 32
BLK = 128
CAP = 64
DEVICES = 128
PAIRS = DEVICES // 2
CHUNK = 16
UE_COUNT = 16
X_COUNT = 4
BF16 = jnp.bfloat16
F32 = jnp.float32


def vmem():
    return pl.BlockSpec(memory_space=pltpu.VMEM)


def take_lanes(values, index):
    return jnp.take_along_axis(values, index, axis=1, mode="promise_in_bounds")


def dot_kernel(order, near, table_ref, gains_ref, out_ref):
    first = order[pl.program_id(0)] * CHUNK

    for row in range(CHUNK):
        block = first + row
        chosen = jnp.concatenate([table_ref[near[block * 4 + k]] for k in range(4)], axis=1)
        weights = gains_ref[row].reshape(4 * BLK, BLK)
        out_ref[0, row] = jnp.dot(chosen, weights, preferred_element_type=F32).astype(out_ref.dtype)


def partial_levels(order, near, table, gains, dtype):
    chunks = order.shape[0]
    return pl.pallas_call(
        dot_kernel,
        grid_spec=pltpu.PrefetchScalarGridSpec(
            num_scalar_prefetch=2,
            grid=(chunks,),
            in_specs=[
                vmem(),
                pl.BlockSpec((CHUNK, 4, BLK, BLK), lambda i, order, near: (order[i], 0, 0, 0)),
            ],
            out_specs=pl.BlockSpec((1, CHUNK, SUB, BLK), lambda i, order, near: (i, 0, 0, 0)),
        ),
        out_shape=jax.ShapeDtypeStruct((chunks, CHUNK, SUB, BLK), dtype),
        compiler_params=pltpu.CompilerParams(vmem_limit_bytes=24 << 20),
        cost_estimate=pl.CostEstimate(
            flops=chunks * CHUNK * 2 * SUB * 4 * BLK * BLK,
            bytes_accessed=chunks * CHUNK * 4 * BLK * BLK * 2,
            transcendentals=0,
        ),
    )(order, near, table, gains)


def half_mask(rows):
    return lax.broadcasted_iota(jnp.int32, (rows, BLK), 1) < CAP


def spread_pair(first, second):
    low = half_mask(first.shape[0])
    return (
        jnp.where(low, first, pltpu.roll(second, CAP, axis=1)),
        jnp.where(low, pltpu.roll(first, CAP, axis=1), second),
    )


def three_parts(value):
    high = value.astype(BF16).astype(F32)
    middle = (value - high).astype(BF16).astype(F32)
    return high, middle, value - high - middle


def route_kernel(with_records, *refs):
    if with_records:
        own, r1, r2, r3, lane_ref, blk_ref, rec_ref, out_ref, levels = refs
    else:
        own, r1, r2, r3, lane_ref, blk_ref, out_ref, levels = refs
    levels[...] = (own[...].astype(F32) + r1[...].astype(F32)) + (
        r2[...].astype(F32) + r3[...].astype(F32)
    )

    def one_pair(pair, carry):
        lane = jnp.broadcast_to(lane_ref[pl.ds(pair, 1), :], (8, BLK))
        blk = jnp.broadcast_to(blk_ref[pl.ds(pair, 1), :], (8, BLK))
        rows = [jnp.zeros((8, BLK), F32) for _ in range(5)]
        for k in range(CHUNK):
            hit = blk == k
            for g in range(4):
                rows[g] = jnp.where(hit, take_lanes(levels[k, 8 * g : 8 * g + 8], lane), rows[g])
            if with_records:
                rows[4] = jnp.where(hit, take_lanes(rec_ref[k], lane), rows[4])
        upper = jnp.concatenate(rows[0:2], axis=0)
        lower = jnp.concatenate(rows[2:4], axis=0)
        even, odd = spread_pair(upper, lower)
        out_ref[2 * pair, 0:16] = even.astype(BF16)
        out_ref[2 * pair + 1, 0:16] = odd.astype(BF16)
        if with_records:
            gain = three_parts(rows[4][0:1])
            average = three_parts(rows[4][1:2])
            cell = rows[4][2:3]
            packed = jnp.concatenate(
                list(gain) + list(average) + [cell] + [jnp.zeros((9, BLK), F32)], axis=0
            )
            out_ref[2 * pair, 16:32] = packed.astype(BF16)
            out_ref[2 * pair + 1, 16:32] = pltpu.roll(packed, CAP, axis=1).astype(BF16)
        return carry

    lax.fori_loop(0, PAIRS, one_pair, 0)


def route(parts, lane, blk, records=None):
    with_records = records is not None
    height = 32 if with_records else 16
    operands = list(parts) + [lane, blk] + ([records] if with_records else [])
    return pl.pallas_call(
        functools.partial(route_kernel, with_records),
        in_specs=[vmem()] * len(operands),
        out_specs=vmem(),
        out_shape=jax.ShapeDtypeStruct((DEVICES, height, BLK), BF16),
        scratch_shapes=[pltpu.VMEM((CHUNK, SUB, BLK), F32)],
        cost_estimate=pl.CostEstimate(flops=8 << 20, bytes_accessed=1 << 20, transcendentals=0),
    )(*operands)


def serve_kernel(first, *refs):
    if first:
        box_ref, power_ref, power_out, low_out, rate_out, inv_out, gain_ref, average_ref, cell_ref = refs
    else:
        (box_ref, power_ref, gain_ref, average_ref, cell_ref, power_out, low_out, rate_out, inv_out) = refs
    power = power_ref[...]
    cells_down = lax.broadcasted_iota(jnp.int32, (BLK, BLK), 0)

    def one_pair(pair):
        even = box_ref[2 * pair].astype(F32)
        odd = box_ref[2 * pair + 1].astype(F32)
        upper, lower = spread_pair(even[0:16], odd[0:16])
        if first:
            low = half_mask(16)
            packed = jnp.where(low, even[16:32], pltpu.roll(odd[16:32], CAP, axis=1))
            gain = packed[0:1] + packed[1:2] + packed[2:3]
            average = packed[3:4] + packed[4:5] + packed[5:6]
            average = jnp.where(gain > 0.0, average, 1.0)
            cell = packed[6:7].astype(jnp.int32)
            gain_ref[pl.ds(pair, 1), :] = gain
            average_ref[pl.ds(pair, 1), :] = average
            cell_ref[pl.ds(pair, 1), :] = cell
        else:
            gain = gain_ref[pl.ds(pair, 1), :]
            average = average_ref[pl.ds(pair, 1), :]
            cell = cell_ref[pl.ds(pair, 1), :]
        levels = jnp.concatenate([upper, lower], axis=0)
        index = jnp.broadcast_to(cell, (8, BLK))
        serving = jnp.concatenate(
            [take_lanes(power[8 * g : 8 * g + 8], index) for g in range(4)], axis=0
        )
        rate = jnp.log1p(gain * serving / (levels + NOISE_FLOOR))
        rate_out[pair] = rate
        metric = rate / average
        high = metric.astype(BF16)
        rest = (metric - high.astype(F32)).astype(BF16)
        onehot = (cells_down == cell).astype(BF16)
        return jnp.concatenate([high, rest], axis=0), onehot

    def step(i, total):
        metric_a, onehot_a = one_pair(2 * i)
        metric_b, onehot_b = one_pair(2 * i + 1)
        metric = jnp.concatenate([metric_a, metric_b], axis=1)
        onehot = jnp.concatenate([onehot_a, onehot_b], axis=1)
        return total + lax.dot_general(
            metric, onehot, (((1,), (1,)), ((), ())), preferred_element_type=F32
        )

    total = lax.fori_loop(0, PAIRS // 2, step, jnp.zeros((2 * SUB, BLK), F32))
    load = total[0:SUB] + total[SUB : 2 * SUB]
    demand = 1.0 + load
    new_power = 0.5 * power + 0.5 * SUB * demand / jnp.sum(demand, axis=0, keepdims=True)
    power_out[...] = new_power
    low = new_power.astype(BF16)
    for k in range(UE_COUNT):
        low_out[k] = low
    inv_out[...] = jnp.where(load > 0.0, 1.0 / load, 0.0)


def serve(box, power, records=None):
    first = records is None
    operands = [box, power] + ([] if first else list(records))
    shapes = [
        jax.ShapeDtypeStruct((SUB, BLK), F32),
        jax.ShapeDtypeStruct((UE_COUNT, SUB, BLK), BF16),
        jax.ShapeDtypeStruct((PAIRS, SUB, BLK), F32),
        jax.ShapeDtypeStruct((SUB, BLK), F32),
    ]
    if first:
        shapes += [
            jax.ShapeDtypeStruct((PAIRS, BLK), F32),
            jax.ShapeDtypeStruct((PAIRS, BLK), F32),
            jax.ShapeDtypeStruct((PAIRS, BLK), jnp.int32),
        ]
    return pl.pallas_call(
        functools.partial(serve_kernel, first),
        in_specs=[vmem()] * len(operands),
        out_specs=[vmem()] * len(shapes),
        out_shape=shapes,
        cost_estimate=pl.CostEstimate(
            flops=1 << 27, bytes_accessed=2 << 20, transcendentals=1 << 18
        ),
    )(*operands)


def average_kernel(last, rate_ref, inv_ref, gain_ref, average_ref, cell_ref, out_ref):
    inv = inv_ref[...]

    def one_pair(pair, carry):
        rate = rate_ref[pair]
        gain = gain_ref[pl.ds(pair, 1), :]
        average = average_ref[pl.ds(pair, 1), :]
        cell = cell_ref[pl.ds(pair, 1), :]
        index = jnp.broadcast_to(cell, (8, BLK))
        spread = jnp.concatenate(
            [take_lanes(inv[8 * g : 8 * g + 8], index) for g in range(4)], axis=0
        )
        served = jnp.sum(rate * rate * spread, axis=0, keepdims=True) / average
        new = KEEP_RATE * average + NEW_RATE * served
        new = jnp.where(gain > 0.0, new, 1.0)
        if last:
            out_ref[2 * pair] = new
            out_ref[2 * pair + 1] = pltpu.roll(new, CAP, axis=1)
        else:
            out_ref[pl.ds(pair, 1), :] = new
        return carry

    lax.fori_loop(0, PAIRS, one_pair, 0)


def update_average(rate, inv, gain, average, cell, last):
    shape = (DEVICES, 1, BLK) if last else (PAIRS, BLK)
    return pl.pallas_call(
        functools.partial(average_kernel, last),
        in_specs=[vmem()] * 5,
        out_specs=vmem(),
        out_shape=jax.ShapeDtypeStruct(shape, F32),
        cost_estimate=pl.CostEstimate(flops=1 << 22, bytes_accessed=1 << 20, transcendentals=0),
    )(rate, inv, gain, average, cell)


def exchange(values, axis):
    return lax.all_to_all(values, axis, split_axis=0, concat_axis=0, tiled=True)


def on_device(gains, near_blocks, serve_block, serve_cell, serve_gain, power_init, avg_init):
    x_here = lax.axis_index("x")
    core_here = lax.axis_index("core")
    everyone = ("ue", "x", "core")
    table = exchange(
        jnp.broadcast_to(power_init.astype(BF16)[None], (UE_COUNT, SUB, BLK)), "ue"
    )
    near = (near_blocks // 8).reshape(-1)
    targets = (x_here + jnp.arange(X_COUNT, dtype=jnp.int32)) % X_COUNT
    order_sibling = 2 * targets + (1 - core_here)
    order_own = 2 * targets + core_here

    destination = serve_block[:, 0]
    rows = destination.shape[0]
    matches = destination[:, None] == jnp.arange(DEVICES, dtype=jnp.int32)[None, :]
    counts = jnp.cumsum(matches.astype(jnp.int32), axis=0)
    position = jnp.sum(jnp.where(matches, counts, 0), axis=1) - 1
    ranks = position[:, None] == jnp.arange(CAP, dtype=jnp.int32)[None, :]
    number = jnp.arange(rows, dtype=jnp.int32)
    located = jnp.concatenate(
        [
            jnp.where(ranks, (number % BLK)[:, None], 0),
            jnp.where(ranks, (number // BLK + 1)[:, None], 0),
        ],
        axis=1,
    ).astype(BF16)
    found = lax.dot_general(
        matches.astype(BF16), located, (((0,), (0,)), ((), ())), preferred_element_type=F32
    ).astype(jnp.int32)
    lane = found[:, :CAP].reshape(PAIRS, BLK)
    blk = (found[:, CAP:] - 1).reshape(PAIRS, BLK)

    home = jnp.stack(
        [serve_gain, avg_init, serve_cell.astype(F32)] + [jnp.zeros_like(serve_gain)] * 5, axis=0
    ).reshape(8, CHUNK, BLK).transpose(1, 0, 2)

    power = power_init
    kept = None
    average = None
    for slot in range(SLOTS):
        away = partial_levels(order_sibling, near, table, gains, BF16)
        arrived = lax.ppermute(away, "core", [(0, 1), (1, 0)])
        mine = partial_levels(order_own, near, table, gains, F32)
        summed = [(mine[k] + arrived[k].astype(F32)).astype(BF16) for k in range(X_COUNT)]
        parts = [summed[0]] + [
            lax.ppermute(summed[k], "x", [(i, (i + k) % X_COUNT) for i in range(X_COUNT)])
            for k in range(1, X_COUNT)
        ]
        box = exchange(route(parts, lane, blk, home if slot == 0 else None), everyone)
        if slot == 0:
            power, low, rate, inv, gain, average, cell = serve(box, power)
        else:
            power, low, rate, inv = serve(box, power, (gain, average, cell))
        last = slot == SLOTS - 1
        if not last:
            table = exchange(low, "ue")
        average = update_average(rate, inv, gain, average, cell, last)
    returned = exchange(average, everyone)[:, 0, :CAP]
    picked = lax.dot_general(
        returned,
        matches.astype(F32),
        (((0,), (1,)), ((), ())),
        precision=lax.Precision.HIGHEST,
        preferred_element_type=F32,
    )
    average_home = jnp.sum(
        jnp.where(position[None, :] == jnp.arange(CAP, dtype=jnp.int32)[:, None], picked, 0.0), axis=0
    )
    return (average_home, power)


def solution(mesh):
    inner = Mesh(mesh.devices.reshape(UE_COUNT, X_COUNT, 2), ("ue", "x", "core"))
    cell = ("x", "core")
    every = ("ue", "x", "core")
    return jax.shard_map(
        on_device,
        mesh=inner,
        in_specs=(
            P("ue", cell, None, None),
            P("ue", cell),
            P(every, None),
            P(every),
            P(every),
            P(None, every),
            P(every),
        ),
        out_specs=(P(every), P(None, every)),
        check_vma=False,
    )
```

```python
import functools
import jax
import jax.numpy as jnp
from jax import lax
from jax.experimental import pallas as pl
from jax.experimental.pallas import tpu as pltpu
from jax.sharding import Mesh, PartitionSpec as P

SLOTS = 4
NOISE_FLOOR = 0.5
KEEP_RATE = 0.7
NEW_RATE = 0.3
SUB = 32
BLK = 128
CAP = 64
DEVICES = 128
PAIRS = DEVICES // 2
CHUNK = 16
UE_COUNT = 16
X_COUNT = 4
BF16 = jnp.bfloat16
F32 = jnp.float32


def vmem():
    return pl.BlockSpec(memory_space=pltpu.VMEM)


def take_lanes(values, index):
    return jnp.take_along_axis(values, index, axis=1, mode="promise_in_bounds")


def dot_kernel(order, near, table_ref, gains_ref, out_ref):
    first = order[pl.program_id(0)] * CHUNK

    for row in range(CHUNK):
        block = first + row
        chosen = jnp.concatenate([table_ref[near[block * 4 + k]] for k in range(4)], axis=1)
        weights = gains_ref[row].reshape(4 * BLK, BLK)
        out_ref[0, row] = jnp.dot(chosen, weights, preferred_element_type=F32).astype(out_ref.dtype)


def partial_levels(order, near, table, gains, dtype):
    chunks = order.shape[0]
    return pl.pallas_call(
        dot_kernel,
        grid_spec=pltpu.PrefetchScalarGridSpec(
            num_scalar_prefetch=2,
            grid=(chunks,),
            in_specs=[
                vmem(),
                pl.BlockSpec((CHUNK, 4, BLK, BLK), lambda i, order, near: (order[i], 0, 0, 0)),
            ],
            out_specs=pl.BlockSpec((1, CHUNK, SUB, BLK), lambda i, order, near: (i, 0, 0, 0)),
        ),
        out_shape=jax.ShapeDtypeStruct((chunks, CHUNK, SUB, BLK), dtype),
        compiler_params=pltpu.CompilerParams(vmem_limit_bytes=12 << 20),
        cost_estimate=pl.CostEstimate(
            flops=chunks * CHUNK * 2 * SUB * 4 * BLK * BLK,
            bytes_accessed=chunks * CHUNK * 4 * BLK * BLK * 2,
            transcendentals=0,
        ),
    )(order, near, table, gains)


def half_mask(rows):
    return lax.broadcasted_iota(jnp.int32, (rows, BLK), 1) < CAP


def three_parts(value):
    high = value.astype(BF16).astype(F32)
    middle = (value - high).astype(BF16).astype(F32)
    return high, middle, value - high - middle


def wide(row):
    return jnp.broadcast_to(row, (8, BLK))


def route_kernel(with_records, start, *refs):
    if with_records:
        own, r1, r2, r3, order_lane, order_blk, slot_lane, slot_part, rec_ref, out_ref, levels, ordered = refs
    else:
        own, r1, r2, r3, order_lane, order_blk, slot_lane, slot_part, out_ref, levels, ordered = refs
    groups = 5 if with_records else 4
    levels[:, 0:SUB] = (own[...].astype(F32) + r1[...].astype(F32)) + (
        r2[...].astype(F32) + r3[...].astype(F32)
    )
    if with_records:
        levels[:, SUB : SUB + 8] = rec_ref[...]
    ordered[CHUNK] = jnp.zeros_like(ordered[CHUNK])

    def sort_step(j, carry):
        lane = wide(order_lane[pl.ds(j, 1), :])
        blk = wide(order_blk[pl.ds(j, 1), :])
        rows = [jnp.zeros((8, BLK), F32) for _ in range(groups)]
        for k in range(CHUNK):
            hit = blk == k
            for g in range(groups):
                rows[g] = jnp.where(hit, take_lanes(levels[k, 8 * g : 8 * g + 8], lane), rows[g])
        for g in range(groups):
            ordered[j, 8 * g : 8 * g + 8] = rows[g]
        return carry

    lax.fori_loop(0, CHUNK, sort_step, 0)

    def one_pair(pair):
        first = start[pair]
        lane = wide(slot_lane[pl.ds(pair, 1), :])
        part = wide(slot_part[pl.ds(pair, 1), :])
        lane_turned = pltpu.roll(lane, CAP, axis=1)
        part_turned = pltpu.roll(part, CAP, axis=1)

        def fetch(g, lane, part):
            near = take_lanes(ordered[first, 8 * g : 8 * g + 8], lane)
            far = take_lanes(ordered[first + 1, 8 * g : 8 * g + 8], lane)
            return jnp.where(part == 0, near, jnp.where(part == 1, far, 0.0))

        upper = jnp.concatenate([fetch(0, lane, part), fetch(1, lane, part)], axis=0)
        lower = jnp.concatenate(
            [fetch(2, lane_turned, part_turned), fetch(3, lane_turned, part_turned)], axis=0
        )
        low = half_mask(16)
        out_ref[2 * pair, 0:16] = jnp.where(low, upper, lower).astype(BF16)
        out_ref[2 * pair + 1, 0:16] = jnp.where(low, lower, upper).astype(BF16)
        if with_records:
            record = fetch(4, lane, part)
            packed = jnp.concatenate(
                list(three_parts(record[0:1]))
                + list(three_parts(record[1:2]))
                + [record[2:3], jnp.zeros((9, BLK), F32)],
                axis=0,
            ).astype(BF16)
            out_ref[2 * pair, 16:32] = packed
            out_ref[2 * pair + 1, 16:32] = packed

    def slot_step(i, carry):
        for k in range(4):
            one_pair(4 * i + k)
        return carry

    lax.fori_loop(0, PAIRS // 4, slot_step, 0)


def route(parts, start, order_lane, order_blk, slot_lane, slot_part, records=None):
    with_records = records is not None
    height = 32 if with_records else 16
    rows = SUB + 8 if with_records else SUB
    operands = list(parts) + [order_lane, order_blk, slot_lane, slot_part]
    operands += [records] if with_records else []
    return pl.pallas_call(
        functools.partial(route_kernel, with_records),
        in_specs=[pl.BlockSpec(memory_space=pltpu.SMEM)] + [vmem()] * len(operands),
        out_specs=vmem(),
        out_shape=jax.ShapeDtypeStruct((DEVICES, height, BLK), BF16),
        scratch_shapes=[
            pltpu.VMEM((CHUNK, rows, BLK), F32),
            pltpu.VMEM((CHUNK + 1, rows, BLK), F32),
        ],
        compiler_params=pltpu.CompilerParams(vmem_limit_bytes=6 << 20),
        cost_estimate=pl.CostEstimate(flops=8 << 20, bytes_accessed=1 << 20, transcendentals=0),
    )(start, *operands)


def new_average(rate, inv, gain, average, cell):
    index = wide(cell)
    spread = jnp.concatenate(
        [take_lanes(inv[8 * g : 8 * g + 8], index) for g in range(4)], axis=0
    )
    served = jnp.sum(rate * rate * spread, axis=0, keepdims=True) / average
    return jnp.where(gain > 0.0, KEEP_RATE * average + NEW_RATE * served, 1.0)


def serve_kernel(first, last, core, *refs):
    refs = list(refs)
    box_ref, power_ref = refs[:2]
    if first:
        power_out, low_out, rate_out, inv_out, gain_ref, average_ref, cell_ref = refs[2:]
    elif last:
        gain_ref, average_ref, cell_ref, power_out, return_out, rate_out = refs[2:]
    else:
        gain_ref, average_ref, cell_ref, power_out, low_out, rate_out, inv_out = refs[2:]
    even_core = core[0] == 0

    def swapped(value):
        top, bottom = value[0:16], value[16:32]
        return jnp.concatenate(
            [jnp.where(even_core, top, bottom), jnp.where(even_core, bottom, top)], axis=0
        )

    power = power_ref[...]
    power_here = swapped(power)
    cells_down = lax.broadcasted_iota(jnp.int32, (BLK, BLK), 0)
    low = half_mask(16)

    def one_pair(pair):
        even = box_ref[2 * pair].astype(F32)
        odd = box_ref[2 * pair + 1].astype(F32)
        upper = jnp.where(low, even[0:16], pltpu.roll(odd[0:16], CAP, axis=1))
        lower = jnp.where(low, pltpu.roll(even[0:16], CAP, axis=1), odd[0:16])
        if first:
            from_low = jnp.where(low, even[16:32], pltpu.roll(odd[16:32], CAP, axis=1))
            from_high = jnp.where(low, pltpu.roll(even[16:32], CAP, axis=1), odd[16:32])
            packed = jnp.where(even_core, from_low, from_high)
            gain = packed[0:1] + packed[1:2] + packed[2:3]
            average = packed[3:4] + packed[4:5] + packed[5:6]
            average = jnp.where(gain > 0.0, average, 1.0)
            cell = packed[6:7].astype(jnp.int32)
            gain_ref[pl.ds(pair, 1), :] = gain
            average_ref[pl.ds(pair, 1), :] = average
            cell_ref[pl.ds(pair, 1), :] = cell
        else:
            gain = gain_ref[pl.ds(pair, 1), :]
            average = average_ref[pl.ds(pair, 1), :]
            cell = cell_ref[pl.ds(pair, 1), :]
        levels = jnp.concatenate([upper, lower], axis=0)
        index = wide(cell)
        serving = jnp.concatenate(
            [take_lanes(power_here[8 * g : 8 * g + 8], index) for g in range(4)], axis=0
        )
        rate = jnp.log1p(gain * serving / (levels + NOISE_FLOOR))
        rate_out[pair] = rate
        metric = rate * (1.0 / average)
        high = metric.astype(BF16)
        rest = (metric - high.astype(F32)).astype(BF16)
        onehot = (cells_down == cell).astype(BF16)
        return jnp.concatenate([high, rest], axis=0), onehot

    def step(i, total):
        pieces = [one_pair(8 * i + k) for k in range(8)]
        metric = jnp.concatenate([piece[0] for piece in pieces], axis=1)
        onehot = jnp.concatenate([piece[1] for piece in pieces], axis=1)
        return total + lax.dot_general(
            metric, onehot, (((1,), (1,)), ((), ())), preferred_element_type=F32
        )

    total = lax.fori_loop(0, PAIRS // 8, step, jnp.zeros((2 * SUB, BLK), F32))
    load_here = total[0:SUB] + total[SUB : 2 * SUB]
    inv = jnp.where(load_here > 0.0, 1.0 / load_here, 0.0)
    demand = 1.0 + swapped(load_here)
    new_power = 0.5 * power + 0.5 * SUB * demand / jnp.sum(demand, axis=0, keepdims=True)
    power_out[...] = new_power
    if not last:
        fresh = new_power.astype(BF16)
        for k in range(UE_COUNT):
            low_out[k] = fresh
        inv_out[...] = inv
        return

    def finish(i, carry):
        for k in range(8):
            pair = 8 * i + k
            gain = gain_ref[pl.ds(pair, 1), :]
            average = average_ref[pl.ds(pair, 1), :]
            cell = cell_ref[pl.ds(pair, 1), :]
            new = new_average(rate_out[pair], inv, gain, average, cell)
            return_out[2 * pair] = new
            return_out[2 * pair + 1] = pltpu.roll(new, CAP, axis=1)
        return carry

    lax.fori_loop(0, PAIRS // 8, finish, 0)


def serve(core, box, power, records=None, last=False):
    first = records is None
    operands = [box, power] + ([] if first else list(records))
    shapes = [jax.ShapeDtypeStruct((SUB, BLK), F32)]
    rates = (PAIRS, SUB, BLK)
    if last:
        shapes += [jax.ShapeDtypeStruct((DEVICES, 1, BLK), F32)]
    else:
        shapes += [
            jax.ShapeDtypeStruct((UE_COUNT, SUB, BLK), BF16),
            jax.ShapeDtypeStruct(rates, F32),
            jax.ShapeDtypeStruct((SUB, BLK), F32),
        ]
    if first:
        shapes += [
            jax.ShapeDtypeStruct((PAIRS, BLK), F32),
            jax.ShapeDtypeStruct((PAIRS, BLK), F32),
            jax.ShapeDtypeStruct((PAIRS, BLK), jnp.int32),
        ]
    return pl.pallas_call(
        functools.partial(serve_kernel, first, last),
        in_specs=[pl.BlockSpec(memory_space=pltpu.SMEM)] + [vmem()] * len(operands),
        out_specs=[vmem()] * len(shapes),
        out_shape=shapes,
        scratch_shapes=[pltpu.VMEM(rates, F32)] if last else [],
        compiler_params=pltpu.CompilerParams(vmem_limit_bytes=8 << 20),
        cost_estimate=pl.CostEstimate(
            flops=1 << 27, bytes_accessed=2 << 20, transcendentals=1 << 18
        ),
    )(core, *operands)


def average_kernel(rate_ref, inv_ref, gain_ref, average_ref, cell_ref, out_ref):
    inv = inv_ref[...]

    def step(i, carry):
        for k in range(8):
            pair = 8 * i + k
            gain = gain_ref[pl.ds(pair, 1), :]
            average = average_ref[pl.ds(pair, 1), :]
            cell = cell_ref[pl.ds(pair, 1), :]
            out_ref[pl.ds(pair, 1), :] = new_average(rate_ref[pair], inv, gain, average, cell)
        return carry

    lax.fori_loop(0, PAIRS // 8, step, 0)


def update_average(rate, inv, gain, average, cell):
    return pl.pallas_call(
        average_kernel,
        in_specs=[vmem()] * 5,
        out_specs=vmem(),
        out_shape=jax.ShapeDtypeStruct((PAIRS, BLK), F32),
        compiler_params=pltpu.CompilerParams(vmem_limit_bytes=4 << 20),
        cost_estimate=pl.CostEstimate(flops=1 << 22, bytes_accessed=1 << 20, transcendentals=0),
    )(rate, inv, gain, average, cell)


def exchange(values, axis):
    return lax.all_to_all(values, axis, split_axis=0, concat_axis=0, tiled=True)


def on_device(gains, near_blocks, serve_block, serve_cell, serve_gain, power_init, avg_init):
    x_here = lax.axis_index("x")
    core_here = lax.axis_index("core")
    everyone = ("ue", "x", "core")
    table = exchange(
        jnp.broadcast_to(power_init.astype(BF16)[None], (UE_COUNT, SUB, BLK)), "ue"
    )
    near = (near_blocks // 8).reshape(-1)
    targets = (x_here + jnp.arange(X_COUNT, dtype=jnp.int32)) % X_COUNT
    order_sibling = 2 * targets + (1 - core_here)
    order_own = 2 * targets + core_here

    destination = serve_block[:, 0]
    rows = destination.shape[0]
    matches = destination[:, None] == jnp.arange(DEVICES, dtype=jnp.int32)[None, :]
    counts = jnp.cumsum(matches.astype(jnp.int32), axis=0)
    position = jnp.sum(jnp.where(matches, counts, 0), axis=1) - 1
    number = jnp.arange(rows, dtype=jnp.int32)
    totals = counts[-1]
    offsets = jnp.cumsum(totals) - totals
    place = position + jnp.sum(jnp.where(matches, offsets[None, :], 0), axis=1)
    lanes = jnp.arange(BLK, dtype=jnp.int32)
    place_lane = (place % BLK)[:, None] == lanes[None, :]
    located = jnp.concatenate(
        [
            jnp.where(place_lane, (number % BLK)[:, None], 0),
            jnp.where(place_lane, (number // BLK)[:, None], 0),
        ],
        axis=1,
    ).astype(BF16)
    place_row = (place // BLK)[:, None] == jnp.arange(CHUNK, dtype=jnp.int32)[None, :]
    found = lax.dot_general(
        place_row.astype(BF16), located, (((0,), (0,)), ((), ())), preferred_element_type=F32
    ).astype(jnp.int32)
    order_lane, order_blk = found[:, :BLK], found[:, BLK:]
    start = offsets.reshape(PAIRS, 2)[:, 0] // BLK
    slot = jnp.arange(CAP, dtype=jnp.int32)
    source = (
        offsets.reshape(PAIRS, 2, 1) + slot[None, None, :] - (start * BLK)[:, None, None]
    )
    filled = slot[None, None, :] < totals.reshape(PAIRS, 2, 1)
    slot_lane = (source % BLK).reshape(PAIRS, BLK)
    slot_part = jnp.where(filled, source // BLK, 2).reshape(PAIRS, BLK)
    routing = (start, order_lane, order_blk, slot_lane, slot_part)

    home = jnp.stack(
        [serve_gain, avg_init, serve_cell.astype(F32)] + [jnp.zeros_like(serve_gain)] * 5, axis=0
    ).reshape(8, CHUNK, BLK).transpose(1, 0, 2)

    table, near, order_sibling, order_own, routing, home = lax.optimization_barrier(
        (table, near, order_sibling, order_own, routing, home)
    )
    power = power_init
    core = core_here.reshape(1)
    for slot in range(SLOTS):
        away = partial_levels(order_sibling, near, table, gains, BF16)
        arrived = lax.ppermute(away, "core", [(0, 1), (1, 0)])
        mine = partial_levels(order_own, near, table, gains, F32)
        summed = [(mine[k] + arrived[k].astype(F32)).astype(BF16) for k in range(X_COUNT)]
        parts = [summed[0]] + [
            lax.ppermute(summed[k], "x", [(i, (i + k) % X_COUNT) for i in range(X_COUNT)])
            for k in range(1, X_COUNT)
        ]
        if slot > 0:
            rate, summed[0] = lax.optimization_barrier((rate, summed[0]))
            average = update_average(rate, inv, gain, average, cell)
            parts[0], average = lax.optimization_barrier((summed[0], average))
        box = exchange(route(parts, *routing, home if slot == 0 else None), everyone)
        if slot == 0:
            power, low, rate, inv, gain, average, cell = serve(core, box, power)
        elif slot < SLOTS - 1:
            power, low, rate, inv = serve(core, box, power, (gain, average, cell))
        else:
            power, leaving = serve(core, box, power, (gain, average, cell), True)
        if slot < SLOTS - 1:
            table = exchange(low, "ue")
    returned = exchange(leaving, everyone)[:, 0, :CAP]
    picked = lax.dot_general(
        returned,
        matches.astype(F32),
        (((0,), (1,)), ((), ())),
        precision=lax.Precision.HIGHEST,
        preferred_element_type=F32,
    )
    average_home = jnp.sum(
        jnp.where(position[None, :] == jnp.arange(CAP, dtype=jnp.int32)[:, None], picked, 0.0), axis=0
    )
    return (average_home, power)


def solution(mesh):
    inner = Mesh(mesh.devices.reshape(UE_COUNT, X_COUNT, 2), ("ue", "x", "core"))
    cell = ("x", "core")
    every = ("ue", "x", "core")
    return jax.shard_map(
        on_device,
        mesh=inner,
        in_specs=(
            P("ue", cell, None, None),
            P("ue", cell),
            P(every, None),
            P(every),
            P(every),
            P(None, every),
            P(every),
        ),
        out_specs=(P(every), P(None, every)),
        check_vma=False,
    )
```

```python
import functools
import jax
import jax.numpy as jnp
from jax import lax
from jax.experimental import pallas as pl
from jax.experimental.pallas import tpu as pltpu
from jax.sharding import Mesh, PartitionSpec as P

SLOTS = 4
NOISE_FLOOR = 0.5
KEEP_RATE = 0.7
NEW_RATE = 0.3
SUB = 32
BLK = 128
CAP = 64
FILLED = 48
DEVICES = 128
PAIRS = DEVICES // 2
CHUNK = 16
HALF = 8
SPLIT = ((0, 1), (1, 3))
UE_COUNT = 16
X_COUNT = 4
HOPS = (2, 1, 3, 0)
BF16 = jnp.bfloat16
F32 = jnp.float32


def vmem():
    return pl.BlockSpec(memory_space=pltpu.VMEM)


def take_lanes(values, index):
    return jnp.take_along_axis(values, index, axis=1, mode="promise_in_bounds")


def block_levels(near, table_ref, block, weights):
    chosen = jnp.concatenate([table_ref[near[block * 4 + k]] for k in range(4)], axis=1)
    return jnp.dot(chosen, weights.reshape(4 * BLK, BLK), preferred_element_type=F32)


def product_cost(blocks):
    return pl.CostEstimate(
        flops=blocks * 2 * SUB * 4 * BLK * BLK,
        bytes_accessed=blocks * 4 * BLK * BLK * 2,
        transcendentals=0,
    )


def first_kernel(order, near, table_ref, gains_ref, out_ref, kept_ref, sems):
    def piece(step):
        chunk, half = step // 2, step % 2
        source = gains_ref.at[pl.ds(order[chunk] * CHUNK + half * HALF, HALF)]
        return pltpu.make_async_copy(
            source, kept_ref.at[chunk, half * HALF : half * HALF + HALF], sems.at[step]
        )

    pieces = [piece(step) for step in range(2 * X_COUNT)]
    for copy in pieces:
        copy.start()
    for step in range(2 * X_COUNT):
        chunk, half = step // 2, step % 2
        pieces[step].wait()
        for row in range(half * HALF, half * HALF + HALF):
            out_ref[chunk, row] = block_levels(
                near, table_ref, order[chunk] * CHUNK + row, kept_ref[chunk, row]
            ).astype(out_ref.dtype)


def first_levels(order, near, table, gains, dtype):
    smem = pl.BlockSpec(memory_space=pltpu.SMEM)
    return pl.pallas_call(
        first_kernel,
        in_specs=[smem, smem, vmem(), pl.BlockSpec(memory_space=pltpu.HBM)],
        out_specs=[vmem(), vmem()],
        out_shape=[
            jax.ShapeDtypeStruct((X_COUNT, CHUNK, SUB, BLK), dtype),
            jax.ShapeDtypeStruct((X_COUNT, CHUNK, 4, BLK, BLK), BF16),
        ],
        scratch_shapes=[pltpu.SemaphoreType.DMA((2 * X_COUNT,))],
        compiler_params=pltpu.CompilerParams(vmem_limit_bytes=20 << 20),
        cost_estimate=product_cost(X_COUNT * CHUNK),
    )(order, near, table, pltpu.with_memory_space_constraint(gains, pltpu.HBM))


def dot_kernel(offset, order, near, table_ref, kept_ref, out_ref):
    first = order[pl.program_id(0) + offset] * CHUNK
    for row in range(CHUNK):
        out_ref[0, row] = block_levels(near, table_ref, first + row, kept_ref[0, row]).astype(
            out_ref.dtype
        )


def partial_levels(offset, chunks, order, near, table, kept, dtype):
    return pl.pallas_call(
        functools.partial(dot_kernel, offset),
        grid_spec=pltpu.PrefetchScalarGridSpec(
            num_scalar_prefetch=2,
            grid=(chunks,),
            in_specs=[
                vmem(),
                pl.BlockSpec((1, CHUNK, 4, BLK, BLK), lambda i, *_: (i + offset, 0, 0, 0, 0)),
            ],
            out_specs=pl.BlockSpec((1, CHUNK, SUB, BLK), lambda i, *_: (i, 0, 0, 0)),
        ),
        out_shape=jax.ShapeDtypeStruct((chunks, CHUNK, SUB, BLK), dtype),
        compiler_params=pltpu.CompilerParams(vmem_limit_bytes=12 << 20),
        cost_estimate=product_cost(chunks * CHUNK),
    )(order, near, table, kept)


def copies_kernel(power_ref, out_ref):
    low = power_ref[...].astype(BF16)
    for k in range(UE_COUNT):
        out_ref[k] = low


def copies(power):
    return pl.pallas_call(
        copies_kernel,
        in_specs=[vmem()],
        out_specs=vmem(),
        out_shape=jax.ShapeDtypeStruct((UE_COUNT, SUB, BLK), BF16),
    )(power)


def half_mask(rows):
    return lax.broadcasted_iota(jnp.int32, (rows, BLK), 1) < CAP


def three_parts(value):
    high = value.astype(BF16).astype(F32)
    middle = (value - high).astype(BF16).astype(F32)
    return high, middle, value - high - middle


def wide(row):
    return jnp.broadcast_to(row, (8, BLK))


def lanes_of(rows):
    return lax.broadcasted_iota(jnp.int32, (rows, BLK), 1)


def with_spare(chunk, packed, base):
    turned = [pltpu.roll(packed, (shift - base) % BLK, axis=1) for shift in (48, 32, 80)]
    lane = lanes_of(16) % CAP
    spare = jnp.where(
        lanes_of(16) < CAP,
        jnp.concatenate(turned[0:2], axis=0),
        jnp.concatenate([turned[2], jnp.zeros((8, BLK), F32)], axis=0),
    )
    return jnp.where(lane >= FILLED, spare, chunk)


def from_spare(chunk, base):
    lane = lanes_of(8) - base
    first = pltpu.roll(chunk[0:8], (80 + base) % BLK, axis=1)
    second = pltpu.roll(chunk[8:16], (96 + base) % BLK, axis=1)
    third = pltpu.roll(chunk[0:8], (48 + base) % BLK, axis=1)
    packed = jnp.where(lane < 16, first, jnp.where(lane < 32, second, third))
    return jnp.where((lane >= 0) & (lane < FILLED), packed, 0.0)


def route_kernel(with_records, start, *refs):
    if with_records:
        own, r1, r2, r3, order_lane, order_blk, slot_lane, slot_part, rec_ref, out_ref, levels, ordered = refs
    else:
        own, r1, r2, r3, order_lane, order_blk, slot_lane, slot_part, out_ref, levels, ordered = refs
    groups = 5 if with_records else 4
    levels[:, 0:SUB] = (own[...].astype(F32) + r1[...].astype(F32)) + (
        r2[...].astype(F32) + r3[...].astype(F32)
    )
    if with_records:
        levels[:, SUB : SUB + 8] = rec_ref[...]
    ordered[CHUNK] = jnp.zeros_like(ordered[CHUNK])

    def sort_step(j, carry):
        lane = wide(order_lane[pl.ds(j, 1), :])
        blk = wide(order_blk[pl.ds(j, 1), :])
        rows = [jnp.zeros((8, BLK), F32) for _ in range(groups)]
        for k in range(CHUNK):
            hit = blk == k
            for g in range(groups):
                rows[g] = jnp.where(hit, take_lanes(levels[k, 8 * g : 8 * g + 8], lane), rows[g])
        for g in range(groups):
            ordered[j, 8 * g : 8 * g + 8] = rows[g]
        return carry

    lax.fori_loop(0, CHUNK, sort_step, 0)

    def one_pair(pair):
        first = start[pair]
        lane = wide(slot_lane[pl.ds(pair, 1), :])
        part = wide(slot_part[pl.ds(pair, 1), :])
        lane_turned = pltpu.roll(lane, CAP, axis=1)
        part_turned = pltpu.roll(part, CAP, axis=1)

        def fetch(g, lane, part):
            near = take_lanes(ordered[first, 8 * g : 8 * g + 8], lane)
            far = take_lanes(ordered[first + 1, 8 * g : 8 * g + 8], lane)
            return jnp.where(part == 0, near, jnp.where(part == 1, far, 0.0))

        upper = jnp.concatenate([fetch(0, lane, part), fetch(1, lane, part)], axis=0)
        lower = jnp.concatenate(
            [fetch(2, lane_turned, part_turned), fetch(3, lane_turned, part_turned)], axis=0
        )
        low = half_mask(16)
        even = jnp.where(low, upper, lower)
        odd = jnp.where(low, lower, upper)
        if with_records:
            record = fetch(4, lane, part)
            packed = jnp.concatenate(
                list(three_parts(record[0:1]))
                + list(three_parts(record[1:2]))
                + [record[2:3], jnp.zeros((1, BLK), F32)],
                axis=0,
            )
            even = with_spare(even, packed, 0)
            odd = with_spare(odd, packed, CAP)
        out_ref[2 * pair] = even.astype(BF16)
        out_ref[2 * pair + 1] = odd.astype(BF16)

    def slot_step(i, carry):
        for k in range(4):
            one_pair(4 * i + k)
        return carry

    lax.fori_loop(0, PAIRS // 4, slot_step, 0)


def route(parts, start, order_lane, order_blk, slot_lane, slot_part, records=None):
    with_records = records is not None
    rows = SUB + 8 if with_records else SUB
    operands = list(parts) + [order_lane, order_blk, slot_lane, slot_part]
    operands += [records] if with_records else []
    return pl.pallas_call(
        functools.partial(route_kernel, with_records),
        in_specs=[pl.BlockSpec(memory_space=pltpu.SMEM)] + [vmem()] * len(operands),
        out_specs=vmem(),
        out_shape=jax.ShapeDtypeStruct((DEVICES, 16, BLK), BF16),
        scratch_shapes=[
            pltpu.VMEM((CHUNK, rows, BLK), F32),
            pltpu.VMEM((CHUNK + 1, rows, BLK), F32),
        ],
        compiler_params=pltpu.CompilerParams(vmem_limit_bytes=6 << 20),
        cost_estimate=pl.CostEstimate(flops=8 << 20, bytes_accessed=1 << 20, transcendentals=0),
    )(start, *operands)


def new_average(rate, inv, gain, average, cell):
    index = wide(cell)
    spread = jnp.concatenate(
        [take_lanes(inv[8 * g : 8 * g + 8], index) for g in range(4)], axis=0
    )
    served = jnp.sum(rate * rate * spread, axis=0, keepdims=True) / average
    return jnp.where(gain > 0.0, KEEP_RATE * average + NEW_RATE * served, 1.0)


def serve_kernel(first, last, core, *refs):
    refs = list(refs)
    box_ref, power_ref = refs[:2]
    if first:
        power_out, low_out, rate_out, inv_out, gain_ref, average_ref, cell_ref = refs[2:]
    elif last:
        gain_ref, average_ref, cell_ref, power_out, return_out, rate_out = refs[2:]
    else:
        gain_ref, average_ref, cell_ref, power_out, low_out, rate_out, inv_out = refs[2:]
    even_core = core[0] == 0

    def swapped(value):
        top, bottom = value[0:16], value[16:32]
        return jnp.concatenate(
            [jnp.where(even_core, top, bottom), jnp.where(even_core, bottom, top)], axis=0
        )

    power = power_ref[...]
    power_here = swapped(power)
    cells_down = lax.broadcasted_iota(jnp.int32, (BLK, BLK), 0)
    low = half_mask(16)

    def one_pair(pair):
        even = box_ref[2 * pair].astype(F32)
        odd = box_ref[2 * pair + 1].astype(F32)
        upper = jnp.where(low, even[0:16], pltpu.roll(odd[0:16], CAP, axis=1))
        lower = jnp.where(low, pltpu.roll(even[0:16], CAP, axis=1), odd[0:16])
        if first:
            packed = from_spare(even, 0) + from_spare(odd, CAP)
            gain = packed[0:1] + packed[1:2] + packed[2:3]
            average = packed[3:4] + packed[4:5] + packed[5:6]
            average = jnp.where(gain > 0.0, average, 1.0)
            cell = packed[6:7].astype(jnp.int32)
            gain_ref[pl.ds(pair, 1), :] = gain
            average_ref[pl.ds(pair, 1), :] = average
            cell_ref[pl.ds(pair, 1), :] = cell
        else:
            gain = gain_ref[pl.ds(pair, 1), :]
            average = average_ref[pl.ds(pair, 1), :]
            cell = cell_ref[pl.ds(pair, 1), :]
        levels = jnp.concatenate([upper, lower], axis=0)
        if first:
            levels = jnp.where(gain > 0.0, levels, 0.0)
        index = wide(cell)
        serving = jnp.concatenate(
            [take_lanes(power_here[8 * g : 8 * g + 8], index) for g in range(4)], axis=0
        )
        rate = jnp.log1p(gain * serving / (levels + NOISE_FLOOR))
        rate_out[pair] = rate
        metric = rate * (1.0 / average)
        high = metric.astype(BF16)
        rest = (metric - high.astype(F32)).astype(BF16)
        onehot = (cells_down == cell).astype(BF16)
        return jnp.concatenate([high, rest], axis=0), onehot

    def step(i, total):
        pieces = [one_pair(8 * i + k) for k in range(8)]
        metric = jnp.concatenate([piece[0] for piece in pieces], axis=1)
        onehot = jnp.concatenate([piece[1] for piece in pieces], axis=1)
        return total + lax.dot_general(
            metric, onehot, (((1,), (1,)), ((), ())), preferred_element_type=F32
        )

    total = lax.fori_loop(0, PAIRS // 8, step, jnp.zeros((2 * SUB, BLK), F32))
    load_here = total[0:SUB] + total[SUB : 2 * SUB]
    inv = jnp.where(load_here > 0.0, 1.0 / load_here, 0.0)
    demand = 1.0 + swapped(load_here)
    new_power = 0.5 * power + 0.5 * SUB * demand / jnp.sum(demand, axis=0, keepdims=True)
    power_out[...] = new_power
    if not last:
        fresh = new_power.astype(BF16)
        for k in range(UE_COUNT):
            low_out[k] = fresh
        inv_out[...] = inv
        return

    def finish(i, carry):
        for k in range(8):
            pair = 8 * i + k
            gain = gain_ref[pl.ds(pair, 1), :]
            average = average_ref[pl.ds(pair, 1), :]
            cell = cell_ref[pl.ds(pair, 1), :]
            new = new_average(rate_out[pair], inv, gain, average, cell)
            return_out[2 * pair] = new
            return_out[2 * pair + 1] = pltpu.roll(new, CAP, axis=1)
        return carry

    lax.fori_loop(0, PAIRS // 8, finish, 0)


def serve(core, box, power, records=None, last=False):
    first = records is None
    operands = [box, power] + ([] if first else list(records))
    shapes = [jax.ShapeDtypeStruct((SUB, BLK), F32)]
    rates = (PAIRS, SUB, BLK)
    if last:
        shapes += [jax.ShapeDtypeStruct((DEVICES, 1, BLK), F32)]
    else:
        shapes += [
            jax.ShapeDtypeStruct((UE_COUNT, SUB, BLK), BF16),
            jax.ShapeDtypeStruct(rates, F32),
            jax.ShapeDtypeStruct((SUB, BLK), F32),
        ]
    if first:
        shapes += [
            jax.ShapeDtypeStruct((PAIRS, BLK), F32),
            jax.ShapeDtypeStruct((PAIRS, BLK), F32),
            jax.ShapeDtypeStruct((PAIRS, BLK), jnp.int32),
        ]
    return pl.pallas_call(
        functools.partial(serve_kernel, first, last),
        in_specs=[pl.BlockSpec(memory_space=pltpu.SMEM)] + [vmem()] * len(operands),
        out_specs=[vmem()] * len(shapes),
        out_shape=shapes,
        scratch_shapes=[pltpu.VMEM(rates, F32)] if last else [],
        compiler_params=pltpu.CompilerParams(vmem_limit_bytes=8 << 20),
        cost_estimate=pl.CostEstimate(
            flops=1 << 27, bytes_accessed=2 << 20, transcendentals=1 << 18
        ),
    )(core, *operands)


def average_kernel(rate_ref, inv_ref, gain_ref, average_ref, cell_ref, out_ref):
    inv = inv_ref[...]

    def step(i, carry):
        for k in range(8):
            pair = 8 * i + k
            gain = gain_ref[pl.ds(pair, 1), :]
            average = average_ref[pl.ds(pair, 1), :]
            cell = cell_ref[pl.ds(pair, 1), :]
            out_ref[pl.ds(pair, 1), :] = new_average(rate_ref[pair], inv, gain, average, cell)
        return carry

    lax.fori_loop(0, PAIRS // 8, step, 0)


def update_average(rate, inv, gain, average, cell):
    return pl.pallas_call(
        average_kernel,
        in_specs=[vmem()] * 5,
        out_specs=vmem(),
        out_shape=jax.ShapeDtypeStruct((PAIRS, BLK), F32),
        compiler_params=pltpu.CompilerParams(vmem_limit_bytes=4 << 20),
        cost_estimate=pl.CostEstimate(flops=1 << 22, bytes_accessed=1 << 20, transcendentals=0),
    )(rate, inv, gain, average, cell)


def exchange(values, axis):
    return lax.all_to_all(values, axis, split_axis=0, concat_axis=0, tiled=True)


def swap_cores(values):
    return lax.ppermute(values, "core", [(0, 1), (1, 0)])


def join(own, arrived):
    return [(own[i] + arrived[i].astype(F32)).astype(BF16) for i in range(own.shape[0])]


def on_device(gains, near_blocks, serve_block, serve_cell, serve_gain, power_init, avg_init):
    x_here = lax.axis_index("x")
    core_here = lax.axis_index("core")
    everyone = ("ue", "x", "core")
    table = exchange(copies(power_init), "ue")
    near = (near_blocks // 8).reshape(-1)
    targets = (x_here + jnp.array(HOPS, dtype=jnp.int32)) % X_COUNT
    order_sibling = 2 * targets + (1 - core_here)
    order_own = 2 * targets + core_here

    destination = serve_block[:, 0]
    rows = destination.shape[0]
    matches = destination[:, None] == jnp.arange(DEVICES, dtype=jnp.int32)[None, :]
    counts = jnp.cumsum(matches.astype(jnp.int32), axis=0)
    position = jnp.sum(jnp.where(matches, counts, 0), axis=1) - 1
    number = jnp.arange(rows, dtype=jnp.int32)
    totals = counts[-1]
    offsets = jnp.cumsum(totals) - totals
    place = position + jnp.sum(jnp.where(matches, offsets[None, :], 0), axis=1)
    lanes = jnp.arange(BLK, dtype=jnp.int32)
    place_lane = (place % BLK)[:, None] == lanes[None, :]
    located = jnp.concatenate(
        [
            jnp.where(place_lane, (number % BLK)[:, None], 0),
            jnp.where(place_lane, (number // BLK)[:, None], 0),
        ],
        axis=1,
    ).astype(BF16)
    place_row = (place // BLK)[:, None] == jnp.arange(CHUNK, dtype=jnp.int32)[None, :]
    found = lax.dot_general(
        place_row.astype(BF16), located, (((0,), (0,)), ((), ())), preferred_element_type=F32
    ).astype(jnp.int32)
    order_lane, order_blk = found[:, :BLK], found[:, BLK:]
    start = offsets.reshape(PAIRS, 2)[:, 0] // BLK
    slot = jnp.arange(CAP, dtype=jnp.int32)
    source = (
        offsets.reshape(PAIRS, 2, 1) + slot[None, None, :] - (start * BLK)[:, None, None]
    )
    filled = slot[None, None, :] < totals.reshape(PAIRS, 2, 1)
    slot_lane = (source % BLK).reshape(PAIRS, BLK)
    slot_part = jnp.where(filled, source // BLK, 2).reshape(PAIRS, BLK)
    routing = (start, order_lane, order_blk, slot_lane, slot_part)

    home = jnp.stack(
        [serve_gain, avg_init, serve_cell.astype(F32)] + [jnp.zeros_like(serve_gain)] * 5, axis=0
    ).reshape(8, CHUNK, BLK).transpose(1, 0, 2)

    table, near, order_sibling, order_own, routing, home = lax.optimization_barrier(
        (table, near, order_sibling, order_own, routing, home)
    )
    power = power_init
    core = core_here.reshape(1)
    for slot in range(SLOTS):
        if slot == 0:
            away, kept_sibling = first_levels(order_sibling, near, table, gains, BF16)
            mine, kept_own = first_levels(order_own, near, table, gains, F32)
            summed = join(mine, swap_cores(away))
        else:
            summed = []
            away = []
            for at, n in SPLIT:
                away.append(partial_levels(at, n, order_sibling, near, table, kept_sibling, BF16))
                table, away[-1] = lax.optimization_barrier((table, away[-1]))
            for (at, n), sent in zip(SPLIT, away):
                own = partial_levels(at, n, order_own, near, table, kept_own, F32)
                summed += join(own, swap_cores(sent))
                table, summed[-1] = lax.optimization_barrier((table, summed[-1]))
        parts = [
            lax.ppermute(value, "x", [(i, (i + hop) % X_COUNT) for i in range(X_COUNT)])
            for value, hop in zip(summed[:3], HOPS)
        ]
        here = summed[3]
        if slot > 0:
            rate, here = lax.optimization_barrier((rate, here))
            average = update_average(rate, inv, gain, average, cell)
            here, average = lax.optimization_barrier((here, average))
        box = exchange(route([here] + parts, *routing, home if slot == 0 else None), everyone)
        if slot == 0:
            power, low, rate, inv, gain, average, cell = serve(core, box, power)
        elif slot < SLOTS - 1:
            power, low, rate, inv = serve(core, box, power, (gain, average, cell))
        else:
            power, leaving = serve(core, box, power, (gain, average, cell), True)
        if slot < SLOTS - 1:
            table = exchange(low, "ue")
    returned = exchange(leaving, everyone)[:, 0, :CAP]
    picked = lax.dot_general(
        returned,
        matches.astype(F32),
        (((0,), (1,)), ((), ())),
        precision=lax.Precision.HIGHEST,
        preferred_element_type=F32,
    )
    average_home = jnp.sum(
        jnp.where(position[None, :] == jnp.arange(CAP, dtype=jnp.int32)[:, None], picked, 0.0), axis=0
    )
    return (average_home, power)


def solution(mesh):
    inner = Mesh(mesh.devices.reshape(UE_COUNT, X_COUNT, 2), ("ue", "x", "core"))
    cell = ("x", "core")
    every = ("ue", "x", "core")
    return jax.shard_map(
        on_device,
        mesh=inner,
        in_specs=(
            P("ue", cell, None, None),
            P("ue", cell),
            P(every, None),
            P(every),
            P(every),
            P(None, every),
            P(every),
        ),
        out_specs=(P(every), P(None, every)),
        check_vma=False,
    )
```

```python
import functools
import jax
import jax.numpy as jnp
from jax import lax
from jax.experimental import pallas as pl
from jax.experimental.pallas import tpu as pltpu
from jax.sharding import Mesh, PartitionSpec as P

SLOTS = 4
NOISE_FLOOR = 0.5
KEEP_RATE = 0.7
NEW_RATE = 0.3
SUB = 32
BLK = 128
CAP = 64
FILLED = 48
DEVICES = 128
PAIRS = DEVICES // 2
CHUNK = 16
HALF = 8
UE_COUNT = 16
X_COUNT = 4
HOPS = (2, 1, 3, 0)
BF16 = jnp.bfloat16
F32 = jnp.float32


def vmem():
    return pl.BlockSpec(memory_space=pltpu.VMEM)


def take_lanes(values, index):
    return jnp.take_along_axis(values, index, axis=1, mode="promise_in_bounds")


def block_levels(near, table_ref, block, weights):
    chosen = jnp.concatenate([table_ref[near[block * 4 + k]] for k in range(4)], axis=1)
    return jnp.dot(chosen, weights.reshape(4 * BLK, BLK), preferred_element_type=F32)


def product_cost(blocks):
    return pl.CostEstimate(
        flops=blocks * 2 * SUB * 4 * BLK * BLK,
        bytes_accessed=blocks * 4 * BLK * BLK * 2,
        transcendentals=0,
    )


def first_kernel(order, near, table_ref, gains_ref, out_ref, kept_ref, sems):
    def piece(step):
        chunk, half = step // 2, step % 2
        source = gains_ref.at[pl.ds(order[chunk] * CHUNK + half * HALF, HALF)]
        return pltpu.make_async_copy(
            source, kept_ref.at[chunk, half * HALF : half * HALF + HALF], sems.at[step]
        )

    pieces = [piece(step) for step in range(2 * X_COUNT)]
    for copy in pieces:
        copy.start()
    for step in range(2 * X_COUNT):
        chunk, half = step // 2, step % 2
        pieces[step].wait()
        for row in range(half * HALF, half * HALF + HALF):
            out_ref[chunk, row] = block_levels(
                near, table_ref, order[chunk] * CHUNK + row, kept_ref[chunk, row]
            ).astype(out_ref.dtype)


def first_levels(order, near, table, gains, dtype):
    smem = pl.BlockSpec(memory_space=pltpu.SMEM)
    return pl.pallas_call(
        first_kernel,
        in_specs=[smem, smem, vmem(), pl.BlockSpec(memory_space=pltpu.HBM)],
        out_specs=[vmem(), vmem()],
        out_shape=[
            jax.ShapeDtypeStruct((X_COUNT, CHUNK, SUB, BLK), dtype),
            jax.ShapeDtypeStruct((X_COUNT, CHUNK, 4, BLK, BLK), BF16),
        ],
        scratch_shapes=[pltpu.SemaphoreType.DMA((2 * X_COUNT,))],
        compiler_params=pltpu.CompilerParams(vmem_limit_bytes=20 << 20),
        cost_estimate=product_cost(X_COUNT * CHUNK),
    )(order, near, table, pltpu.with_memory_space_constraint(gains, pltpu.HBM))


def dot_kernel(order, near, table_ref, kept_ref, out_ref):
    for chunk in range(X_COUNT):
        for row in range(CHUNK):
            out_ref[chunk, row] = block_levels(
                near, table_ref, order[chunk] * CHUNK + row, kept_ref[chunk, row]
            ).astype(out_ref.dtype)


def partial_levels(order, near, table, kept, dtype):
    smem = pl.BlockSpec(memory_space=pltpu.SMEM)
    return pl.pallas_call(
        dot_kernel,
        in_specs=[smem, smem, vmem(), vmem()],
        out_specs=vmem(),
        out_shape=jax.ShapeDtypeStruct((X_COUNT, CHUNK, SUB, BLK), dtype),
        compiler_params=pltpu.CompilerParams(vmem_limit_bytes=12 << 20),
        cost_estimate=product_cost(X_COUNT * CHUNK),
    )(order, near, table, kept)


def copies_kernel(power_ref, out_ref):
    low = power_ref[...].astype(BF16)
    for k in range(UE_COUNT):
        out_ref[k] = low


def copies(power):
    return pl.pallas_call(
        copies_kernel,
        in_specs=[vmem()],
        out_specs=vmem(),
        out_shape=jax.ShapeDtypeStruct((UE_COUNT, SUB, BLK), BF16),
    )(power)


def half_mask(rows):
    return lax.broadcasted_iota(jnp.int32, (rows, BLK), 1) < CAP


def three_parts(value):
    high = value.astype(BF16).astype(F32)
    middle = (value - high).astype(BF16).astype(F32)
    return high, middle, value - high - middle


def wide(row):
    return jnp.broadcast_to(row, (8, BLK))


def lanes_of(rows):
    return lax.broadcasted_iota(jnp.int32, (rows, BLK), 1)


def with_spare(chunk, packed, base):
    turned = [pltpu.roll(packed, (shift - base) % BLK, axis=1) for shift in (48, 32, 80)]
    lane = lanes_of(16) % CAP
    spare = jnp.where(
        lanes_of(16) < CAP,
        jnp.concatenate(turned[0:2], axis=0),
        jnp.concatenate([turned[2], jnp.zeros((8, BLK), F32)], axis=0),
    )
    return jnp.where(lane >= FILLED, spare, chunk)


def from_spare(chunk, base):
    lane = lanes_of(8) - base
    first = pltpu.roll(chunk[0:8], (80 + base) % BLK, axis=1)
    second = pltpu.roll(chunk[8:16], (96 + base) % BLK, axis=1)
    third = pltpu.roll(chunk[0:8], (48 + base) % BLK, axis=1)
    packed = jnp.where(lane < 16, first, jnp.where(lane < 32, second, third))
    return jnp.where((lane >= 0) & (lane < FILLED), packed, 0.0)


def route_kernel(with_records, start, *refs):
    if with_records:
        own, r1, r2, r3, order_lane, order_blk, slot_lane, slot_part, rec_ref, out_ref, levels, ordered = refs
    else:
        own, r1, r2, r3, order_lane, order_blk, slot_lane, slot_part, out_ref, levels, ordered = refs
    groups = 5 if with_records else 4
    levels[:, 0:SUB] = (own[...].astype(F32) + r1[...].astype(F32)) + (
        r2[...].astype(F32) + r3[...].astype(F32)
    )
    if with_records:
        levels[:, SUB : SUB + 8] = rec_ref[...]
    ordered[CHUNK] = jnp.zeros_like(ordered[CHUNK])

    for j in range(CHUNK):
        lane = wide(order_lane[j : j + 1, :])
        blk = wide(order_blk[j : j + 1, :])
        rows = [jnp.zeros((8, BLK), F32) for _ in range(groups)]
        for k in range(CHUNK):
            hit = blk == k
            for g in range(groups):
                rows[g] = jnp.where(hit, take_lanes(levels[k, 8 * g : 8 * g + 8], lane), rows[g])
        for g in range(groups):
            ordered[j, 8 * g : 8 * g + 8] = rows[g]

    def one_pair(pair):
        first = start[pair]
        lane = wide(slot_lane[pl.ds(pair, 1), :])
        part = wide(slot_part[pl.ds(pair, 1), :])
        lane_turned = pltpu.roll(lane, CAP, axis=1)
        part_turned = pltpu.roll(part, CAP, axis=1)

        def fetch(g, lane, part):
            near = take_lanes(ordered[first, 8 * g : 8 * g + 8], lane)
            far = take_lanes(ordered[first + 1, 8 * g : 8 * g + 8], lane)
            return jnp.where(part == 0, near, jnp.where(part == 1, far, 0.0))

        upper = jnp.concatenate([fetch(0, lane, part), fetch(1, lane, part)], axis=0)
        lower = jnp.concatenate(
            [fetch(2, lane_turned, part_turned), fetch(3, lane_turned, part_turned)], axis=0
        )
        low = half_mask(16)
        even = jnp.where(low, upper, lower)
        odd = jnp.where(low, lower, upper)
        if with_records:
            record = fetch(4, lane, part)
            packed = jnp.concatenate(
                list(three_parts(record[0:1]))
                + list(three_parts(record[1:2]))
                + [record[2:3], jnp.zeros((1, BLK), F32)],
                axis=0,
            )
            even = with_spare(even, packed, 0)
            odd = with_spare(odd, packed, CAP)
        out_ref[2 * pair] = even.astype(BF16)
        out_ref[2 * pair + 1] = odd.astype(BF16)

    def slot_step(i, carry):
        for k in range(16):
            one_pair(16 * i + k)
        return carry

    lax.fori_loop(0, PAIRS // 16, slot_step, 0)


def route(parts, start, order_lane, order_blk, slot_lane, slot_part, records=None):
    with_records = records is not None
    rows = SUB + 8 if with_records else SUB
    operands = list(parts) + [order_lane, order_blk, slot_lane, slot_part]
    operands += [records] if with_records else []
    return pl.pallas_call(
        functools.partial(route_kernel, with_records),
        in_specs=[pl.BlockSpec(memory_space=pltpu.SMEM)] + [vmem()] * len(operands),
        out_specs=vmem(),
        out_shape=jax.ShapeDtypeStruct((DEVICES, 16, BLK), BF16),
        scratch_shapes=[
            pltpu.VMEM((CHUNK, rows, BLK), F32),
            pltpu.VMEM((CHUNK + 1, rows, BLK), F32),
        ],
        compiler_params=pltpu.CompilerParams(vmem_limit_bytes=6 << 20),
        cost_estimate=pl.CostEstimate(flops=8 << 20, bytes_accessed=1 << 20, transcendentals=0),
    )(start, *operands)


def new_average(rate, inv, gain, average, cell):
    index = wide(cell)
    spread = jnp.concatenate(
        [take_lanes(inv[8 * g : 8 * g + 8], index) for g in range(4)], axis=0
    )
    served = jnp.sum(rate * rate * spread, axis=0, keepdims=True) / average
    return jnp.where(gain > 0.0, KEEP_RATE * average + NEW_RATE * served, 1.0)


def serve_kernel(first, last, core, *refs):
    refs = list(refs)
    box_ref, power_ref = refs[:2]
    if first:
        power_out, low_out, rate_out, inv_out, gain_ref, average_ref, cell_ref = refs[2:]
    elif last:
        gain_ref, average_ref, cell_ref, power_out, return_out, rate_out = refs[2:]
    else:
        gain_ref, average_ref, cell_ref, power_out, low_out, rate_out, inv_out = refs[2:]
    even_core = core[0] == 0

    def swapped(value):
        top, bottom = value[0:16], value[16:32]
        return jnp.concatenate(
            [jnp.where(even_core, top, bottom), jnp.where(even_core, bottom, top)], axis=0
        )

    power = power_ref[...]
    power_here = swapped(power)
    cells_down = lax.broadcasted_iota(jnp.int32, (BLK, BLK), 0)
    low = half_mask(16)

    def one_pair(pair):
        even = box_ref[2 * pair].astype(F32)
        odd = box_ref[2 * pair + 1].astype(F32)
        upper = jnp.where(low, even[0:16], pltpu.roll(odd[0:16], CAP, axis=1))
        lower = jnp.where(low, pltpu.roll(even[0:16], CAP, axis=1), odd[0:16])
        if first:
            packed = from_spare(even, 0) + from_spare(odd, CAP)
            gain = packed[0:1] + packed[1:2] + packed[2:3]
            average = packed[3:4] + packed[4:5] + packed[5:6]
            average = jnp.where(gain > 0.0, average, 1.0)
            cell = packed[6:7].astype(jnp.int32)
            gain_ref[pl.ds(pair, 1), :] = gain
            average_ref[pl.ds(pair, 1), :] = average
            cell_ref[pl.ds(pair, 1), :] = cell
        else:
            gain = gain_ref[pl.ds(pair, 1), :]
            average = average_ref[pl.ds(pair, 1), :]
            cell = cell_ref[pl.ds(pair, 1), :]
        levels = jnp.concatenate([upper, lower], axis=0)
        if first:
            levels = jnp.where(gain > 0.0, levels, 0.0)
        index = wide(cell)
        serving = jnp.concatenate(
            [take_lanes(power_here[8 * g : 8 * g + 8], index) for g in range(4)], axis=0
        )
        rate = jnp.log1p(gain * serving / (levels + NOISE_FLOOR))
        rate_out[pair] = rate
        metric = rate * (1.0 / average)
        high = metric.astype(BF16)
        rest = (metric - high.astype(F32)).astype(BF16)
        onehot = (cells_down == cell).astype(BF16)
        return jnp.concatenate([high, rest], axis=0), onehot

    def step(i, total):
        pieces = [one_pair(8 * i + k) for k in range(8)]
        metric = jnp.concatenate([piece[0] for piece in pieces], axis=1)
        onehot = jnp.concatenate([piece[1] for piece in pieces], axis=1)
        return total + lax.dot_general(
            metric, onehot, (((1,), (1,)), ((), ())), preferred_element_type=F32
        )

    total = lax.fori_loop(0, PAIRS // 8, step, jnp.zeros((2 * SUB, BLK), F32))
    load_here = total[0:SUB] + total[SUB : 2 * SUB]
    inv = jnp.where(load_here > 0.0, 1.0 / load_here, 0.0)
    demand = 1.0 + swapped(load_here)
    new_power = 0.5 * power + 0.5 * SUB * demand / jnp.sum(demand, axis=0, keepdims=True)
    power_out[...] = new_power
    if not last:
        fresh = new_power.astype(BF16)
        for k in range(UE_COUNT):
            low_out[k] = fresh
        inv_out[...] = inv
        return

    def finish(i, carry):
        for k in range(8):
            pair = 8 * i + k
            gain = gain_ref[pl.ds(pair, 1), :]
            average = average_ref[pl.ds(pair, 1), :]
            cell = cell_ref[pl.ds(pair, 1), :]
            new = new_average(rate_out[pair], inv, gain, average, cell)
            return_out[2 * pair] = new
            return_out[2 * pair + 1] = pltpu.roll(new, CAP, axis=1)
        return carry

    lax.fori_loop(0, PAIRS // 8, finish, 0)


def serve(core, box, power, records=None, last=False):
    first = records is None
    operands = [box, power] + ([] if first else list(records))
    shapes = [jax.ShapeDtypeStruct((SUB, BLK), F32)]
    rates = (PAIRS, SUB, BLK)
    if last:
        shapes += [jax.ShapeDtypeStruct((DEVICES, 1, BLK), F32)]
    else:
        shapes += [
            jax.ShapeDtypeStruct((UE_COUNT, SUB, BLK), BF16),
            jax.ShapeDtypeStruct(rates, F32),
            jax.ShapeDtypeStruct((SUB, BLK), F32),
        ]
    if first:
        shapes += [
            jax.ShapeDtypeStruct((PAIRS, BLK), F32),
            jax.ShapeDtypeStruct((PAIRS, BLK), F32),
            jax.ShapeDtypeStruct((PAIRS, BLK), jnp.int32),
        ]
    return pl.pallas_call(
        functools.partial(serve_kernel, first, last),
        in_specs=[pl.BlockSpec(memory_space=pltpu.SMEM)] + [vmem()] * len(operands),
        out_specs=[vmem()] * len(shapes),
        out_shape=shapes,
        scratch_shapes=[pltpu.VMEM(rates, F32)] if last else [],
        compiler_params=pltpu.CompilerParams(vmem_limit_bytes=8 << 20),
        cost_estimate=pl.CostEstimate(
            flops=1 << 27, bytes_accessed=2 << 20, transcendentals=1 << 18
        ),
    )(core, *operands)


def average_kernel(rate_ref, inv_ref, gain_ref, average_ref, cell_ref, out_ref):
    inv = inv_ref[...]

    def step(i, carry):
        for k in range(8):
            pair = 8 * i + k
            gain = gain_ref[pl.ds(pair, 1), :]
            average = average_ref[pl.ds(pair, 1), :]
            cell = cell_ref[pl.ds(pair, 1), :]
            out_ref[pl.ds(pair, 1), :] = new_average(rate_ref[pair], inv, gain, average, cell)
        return carry

    lax.fori_loop(0, PAIRS // 8, step, 0)


def update_average(rate, inv, gain, average, cell):
    return pl.pallas_call(
        average_kernel,
        in_specs=[vmem()] * 5,
        out_specs=vmem(),
        out_shape=jax.ShapeDtypeStruct((PAIRS, BLK), F32),
        compiler_params=pltpu.CompilerParams(vmem_limit_bytes=4 << 20),
        cost_estimate=pl.CostEstimate(flops=1 << 22, bytes_accessed=1 << 20, transcendentals=0),
    )(rate, inv, gain, average, cell)


def exchange(values, axis):
    return lax.all_to_all(values, axis, split_axis=0, concat_axis=0, tiled=True)


def swap_cores(values):
    return lax.ppermute(values, "core", [(0, 1), (1, 0)])


def join(own, arrived):
    return [(own[i] + arrived[i].astype(F32)).astype(BF16) for i in range(own.shape[0])]


def on_device(gains, near_blocks, serve_block, serve_cell, serve_gain, power_init, avg_init):
    x_here = lax.axis_index("x")
    core_here = lax.axis_index("core")
    everyone = ("ue", "x", "core")
    table = exchange(copies(power_init), "ue")
    near = (near_blocks // 8).reshape(-1)
    targets = (x_here + jnp.array(HOPS, dtype=jnp.int32)) % X_COUNT
    order_sibling = 2 * targets + (1 - core_here)
    order_own = 2 * targets + core_here

    destination = serve_block[:, 0]
    rows = destination.shape[0]
    matches = destination[:, None] == jnp.arange(DEVICES, dtype=jnp.int32)[None, :]
    counts = jnp.cumsum(matches.astype(jnp.int32), axis=0)
    position = jnp.sum(jnp.where(matches, counts, 0), axis=1) - 1
    number = jnp.arange(rows, dtype=jnp.int32)
    totals = counts[-1]
    offsets = jnp.cumsum(totals) - totals
    place = position + jnp.sum(jnp.where(matches, offsets[None, :], 0), axis=1)
    lanes = jnp.arange(BLK, dtype=jnp.int32)
    place_lane = (place % BLK)[:, None] == lanes[None, :]
    located = jnp.concatenate(
        [
            jnp.where(place_lane, (number % BLK)[:, None], 0),
            jnp.where(place_lane, (number // BLK)[:, None], 0),
        ],
        axis=1,
    ).astype(BF16)
    place_row = (place // BLK)[:, None] == jnp.arange(CHUNK, dtype=jnp.int32)[None, :]
    found = lax.dot_general(
        place_row.astype(BF16), located, (((0,), (0,)), ((), ())), preferred_element_type=F32
    ).astype(jnp.int32)
    order_lane, order_blk = found[:, :BLK], found[:, BLK:]
    start = jnp.minimum(offsets.reshape(PAIRS, 2)[:, 0] // BLK, CHUNK - 1)
    slot = jnp.arange(CAP, dtype=jnp.int32)
    source = (
        offsets.reshape(PAIRS, 2, 1) + slot[None, None, :] - (start * BLK)[:, None, None]
    )
    filled = slot[None, None, :] < totals.reshape(PAIRS, 2, 1)
    slot_lane = (source % BLK).reshape(PAIRS, BLK)
    slot_part = jnp.where(filled, source // BLK, 2).reshape(PAIRS, BLK)
    routing = (start, order_lane, order_blk, slot_lane, slot_part)

    home = jnp.stack(
        [serve_gain, avg_init, serve_cell.astype(F32)] + [jnp.zeros_like(serve_gain)] * 5, axis=0
    ).reshape(8, CHUNK, BLK).transpose(1, 0, 2)

    table, near, order_sibling, order_own, routing, home = lax.optimization_barrier(
        (table, near, order_sibling, order_own, routing, home)
    )
    power = power_init
    core = core_here.reshape(1)
    for slot in range(SLOTS):
        if slot == 0:
            away, kept_sibling = first_levels(order_sibling, near, table, gains, BF16)
            mine, kept_own = first_levels(order_own, near, table, gains, F32)
            summed = join(mine, swap_cores(away))
        else:
            away = partial_levels(order_sibling, near, table, kept_sibling, BF16)
            mine = partial_levels(order_own, near, table, kept_own, F32)
            summed = join(mine, swap_cores(away))
        parts = [
            lax.ppermute(value, "x", [(i, (i + hop) % X_COUNT) for i in range(X_COUNT)])
            for value, hop in zip(summed[:3], HOPS)
        ]
        here = summed[3]
        if slot > 0:
            rate, here = lax.optimization_barrier((rate, here))
            average = update_average(rate, inv, gain, average, cell)
            here, average = lax.optimization_barrier((here, average))
        box = exchange(route([here] + parts, *routing, home if slot == 0 else None), everyone)
        if slot == 0:
            power, low, rate, inv, gain, average, cell = serve(core, box, power)
        elif slot < SLOTS - 1:
            power, low, rate, inv = serve(core, box, power, (gain, average, cell))
        else:
            power, leaving = serve(core, box, power, (gain, average, cell), True)
        if slot < SLOTS - 1:
            table = exchange(low, "ue")
    returned = exchange(leaving, everyone)[:, 0, :CAP]
    picked = lax.dot_general(
        returned,
        matches.astype(F32),
        (((0,), (1,)), ((), ())),
        precision=lax.Precision.HIGHEST,
        preferred_element_type=F32,
    )
    average_home = jnp.sum(
        jnp.where(position[None, :] == jnp.arange(CAP, dtype=jnp.int32)[:, None], picked, 0.0), axis=0
    )
    return (average_home, power)


def solution(mesh):
    inner = Mesh(mesh.devices.reshape(UE_COUNT, X_COUNT, 2), ("ue", "x", "core"))
    cell = ("x", "core")
    every = ("ue", "x", "core")
    return jax.shard_map(
        on_device,
        mesh=inner,
        in_specs=(
            P("ue", cell, None, None),
            P("ue", cell),
            P(every, None),
            P(every),
            P(every),
            P(None, every),
            P(every),
        ),
        out_specs=(P(every), P(None, every)),
        check_vma=False,
    )
```

```python
import functools
import jax
import jax.numpy as jnp
from jax import lax
from jax.experimental import pallas as pl
from jax.experimental.pallas import tpu as pltpu
from jax.sharding import Mesh, PartitionSpec as P

SLOTS = 4
NOISE_FLOOR = 0.5
KEEP_RATE = 0.7
NEW_RATE = 0.3
SUB = 32
BLK = 128
CAP = 64
FILLED = 48
DEVICES = 128
PAIRS = DEVICES // 2
CHUNK = 16
HALF = 8
BLOCKS = 128
SPLIT = ((0,), (1, 2, 3))
UE_COUNT = 16
X_COUNT = 4
HOPS = (2, 1, 3, 0)
BF16 = jnp.bfloat16
F32 = jnp.float32


def vmem():
    return pl.BlockSpec(memory_space=pltpu.VMEM)


def take_lanes(values, index):
    return jnp.take_along_axis(values, index, axis=1, mode="promise_in_bounds")


def block_levels(near, table_ref, block, weights):
    chosen = jnp.concatenate([table_ref[near[k * BLOCKS + block] >> 3] for k in range(4)], axis=1)
    return jnp.dot(chosen, weights.reshape(4 * BLK, BLK), preferred_element_type=F32)


def product_cost(blocks):
    return pl.CostEstimate(
        flops=blocks * 2 * SUB * 4 * BLK * BLK,
        bytes_accessed=blocks * 4 * BLK * BLK * 2,
        transcendentals=0,
    )


def block_order(own):
    core = lax.axis_index("core")
    core = core if own else 1 - core
    return [2 * ((lax.axis_index("x") + hop) % X_COUNT) + core for hop in HOPS]


def first_kernel(own, near, table_ref, gains_ref, out_ref, kept_ref, sems):
    order = block_order(own)

    def piece(step):
        chunk, half = step // 2, step % 2
        source = gains_ref.at[pl.ds(order[chunk] * CHUNK + half * HALF, HALF)]
        return pltpu.make_async_copy(
            source, kept_ref.at[chunk, half * HALF : half * HALF + HALF], sems.at[step]
        )

    pieces = [piece(step) for step in range(2 * X_COUNT)]
    for copy in pieces:
        copy.start()
    for step in range(2 * X_COUNT):
        chunk, half = step // 2, step % 2
        pieces[step].wait()
        for row in range(half * HALF, half * HALF + HALF):
            out_ref[chunk, row] = block_levels(
                near, table_ref, order[chunk] * CHUNK + row, kept_ref[chunk, row]
            ).astype(out_ref.dtype)


def first_levels(own, near, table, gains, dtype):
    smem = pl.BlockSpec(memory_space=pltpu.SMEM)
    return pl.pallas_call(
        functools.partial(first_kernel, own),
        in_specs=[smem, vmem(), pl.BlockSpec(memory_space=pltpu.HBM)],
        out_specs=[vmem(), vmem()],
        out_shape=[
            jax.ShapeDtypeStruct((X_COUNT, CHUNK, SUB, BLK), dtype),
            jax.ShapeDtypeStruct((X_COUNT, CHUNK, 4, BLK, BLK), BF16),
        ],
        scratch_shapes=[pltpu.SemaphoreType.DMA((2 * X_COUNT,))],
        compiler_params=pltpu.CompilerParams(vmem_limit_bytes=20 << 20),
        cost_estimate=product_cost(X_COUNT * CHUNK),
    )(near, table, pltpu.with_memory_space_constraint(gains, pltpu.HBM))


def dot_kernel(own, groups, near, table_ref, kept_ref, *out_refs):
    order = block_order(own)
    for chunks, out_ref in zip(groups, out_refs):
        for place, chunk in enumerate(chunks):
            for row in range(CHUNK):
                out_ref[place, row] = block_levels(
                    near, table_ref, order[chunk] * CHUNK + row, kept_ref[chunk, row]
                ).astype(out_ref.dtype)


def partial_levels(own, groups, near, table, kept, dtype):
    smem = pl.BlockSpec(memory_space=pltpu.SMEM)
    return pl.pallas_call(
        functools.partial(dot_kernel, own, groups),
        in_specs=[smem, vmem(), vmem()],
        out_specs=[vmem() for _ in groups],
        out_shape=[
            jax.ShapeDtypeStruct((len(chunks), CHUNK, SUB, BLK), dtype) for chunks in groups
        ],
        compiler_params=pltpu.CompilerParams(vmem_limit_bytes=12 << 20),
        cost_estimate=pl.CostEstimate(flops=1 << 10, bytes_accessed=1 << 10, transcendentals=0),
    )(near, table, kept)


def copies_kernel(power_ref, out_ref):
    low = power_ref[...].astype(BF16)
    for k in range(UE_COUNT):
        out_ref[k] = low


def copies(power):
    return pl.pallas_call(
        copies_kernel,
        in_specs=[vmem()],
        out_specs=vmem(),
        out_shape=jax.ShapeDtypeStruct((UE_COUNT, SUB, BLK), BF16),
    )(power)


def half_mask(rows):
    return lax.broadcasted_iota(jnp.int32, (rows, BLK), 1) < CAP


def three_parts(value):
    high = value.astype(BF16).astype(F32)
    middle = (value - high).astype(BF16).astype(F32)
    return high, middle, value - high - middle


def wide(row):
    return jnp.broadcast_to(row, (8, BLK))


def lanes_of(rows):
    return lax.broadcasted_iota(jnp.int32, (rows, BLK), 1)


def with_spare(chunk, packed, base):
    turned = [pltpu.roll(packed, (shift - base) % BLK, axis=1) for shift in (48, 32, 80)]
    lane = lanes_of(16) % CAP
    spare = jnp.where(
        lanes_of(16) < CAP,
        jnp.concatenate(turned[0:2], axis=0),
        jnp.concatenate([turned[2], jnp.zeros((8, BLK), F32)], axis=0),
    )
    return jnp.where(lane >= FILLED, spare, chunk)


def from_spare(chunk, base):
    lane = lanes_of(8) - base
    first = pltpu.roll(chunk[0:8], (80 + base) % BLK, axis=1)
    second = pltpu.roll(chunk[8:16], (96 + base) % BLK, axis=1)
    third = pltpu.roll(chunk[0:8], (48 + base) % BLK, axis=1)
    packed = jnp.where(lane < 16, first, jnp.where(lane < 32, second, third))
    return jnp.where((lane >= 0) & (lane < FILLED), packed, 0.0)


def route_kernel(with_records, start, *refs):
    if with_records:
        own, r1, r2, r3, order_lane, order_blk, slot_lane, slot_part, gains, averages, cells, out_ref, levels, ordered = refs
    else:
        own, r1, r2, r3, order_lane, order_blk, slot_lane, slot_part, out_ref, levels, ordered = refs
    groups = 5 if with_records else 4
    levels[:, 0:SUB] = (own[...].astype(F32) + r1[...].astype(F32)) + (
        r2[...].astype(F32) + r3[...].astype(F32)
    )
    if with_records:
        levels[:, SUB : SUB + 8] = jnp.zeros((CHUNK, 8, BLK), F32)
        for k in range(CHUNK):
            levels[k, SUB : SUB + 1] = gains[k : k + 1]
            levels[k, SUB + 1 : SUB + 2] = averages[k : k + 1]
            levels[k, SUB + 2 : SUB + 3] = cells[k : k + 1].astype(F32)
    ordered[CHUNK] = jnp.zeros_like(ordered[CHUNK])

    for j in range(CHUNK):
        lane = wide(order_lane[j : j + 1, :])
        blk = wide(order_blk[j : j + 1, :])
        rows = [jnp.zeros((8, BLK), F32) for _ in range(groups)]
        for k in range(CHUNK):
            hit = blk == k
            for g in range(groups):
                rows[g] = jnp.where(hit, take_lanes(levels[k, 8 * g : 8 * g + 8], lane), rows[g])
        for g in range(groups):
            ordered[j, 8 * g : 8 * g + 8] = rows[g]

    def one_pair(pair):
        first = start[pair]
        lane = wide(slot_lane[pl.ds(pair, 1), :])
        part = wide(slot_part[pl.ds(pair, 1), :])
        lane_turned = pltpu.roll(lane, CAP, axis=1)
        part_turned = pltpu.roll(part, CAP, axis=1)

        def fetch(g, lane, part):
            near = take_lanes(ordered[first, 8 * g : 8 * g + 8], lane)
            far = take_lanes(ordered[first + 1, 8 * g : 8 * g + 8], lane)
            return jnp.where(part == 0, near, jnp.where(part == 1, far, 0.0))

        upper = jnp.concatenate([fetch(0, lane, part), fetch(1, lane, part)], axis=0)
        lower = jnp.concatenate(
            [fetch(2, lane_turned, part_turned), fetch(3, lane_turned, part_turned)], axis=0
        )
        low = half_mask(16)
        even = jnp.where(low, upper, lower)
        odd = jnp.where(low, lower, upper)
        if with_records:
            record = fetch(4, lane, part)
            packed = jnp.concatenate(
                list(three_parts(record[0:1]))
                + list(three_parts(record[1:2]))
                + [record[2:3], jnp.zeros((1, BLK), F32)],
                axis=0,
            )
            even = with_spare(even, packed, 0)
            odd = with_spare(odd, packed, CAP)
        out_ref[2 * pair] = even.astype(BF16)
        out_ref[2 * pair + 1] = odd.astype(BF16)

    def slot_step(i, carry):
        for k in range(8):
            one_pair(8 * i + k)
        return carry

    lax.fori_loop(0, PAIRS // 8, slot_step, 0)


def route(parts, start, order_lane, order_blk, slot_lane, slot_part, records=None):
    with_records = records is not None
    rows = SUB + 8 if with_records else SUB
    operands = list(parts) + [order_lane, order_blk, slot_lane, slot_part]
    operands += list(records) if with_records else []
    return pl.pallas_call(
        functools.partial(route_kernel, with_records),
        in_specs=[pl.BlockSpec(memory_space=pltpu.SMEM)] + [vmem()] * len(operands),
        out_specs=vmem(),
        out_shape=jax.ShapeDtypeStruct((DEVICES, 16, BLK), BF16),
        scratch_shapes=[
            pltpu.VMEM((CHUNK, rows, BLK), F32),
            pltpu.VMEM((CHUNK + 1, rows, BLK), F32),
        ],
        compiler_params=pltpu.CompilerParams(vmem_limit_bytes=6 << 20),
        cost_estimate=pl.CostEstimate(flops=8 << 20, bytes_accessed=1 << 20, transcendentals=0),
    )(start, *operands)


def new_average(rate, inv, gain, average, cell):
    index = wide(cell)
    spread = jnp.concatenate(
        [take_lanes(inv[8 * g : 8 * g + 8], index) for g in range(4)], axis=0
    )
    served = jnp.sum(rate * rate * spread, axis=0, keepdims=True) / average
    return jnp.where(gain > 0.0, KEEP_RATE * average + NEW_RATE * served, 1.0)


def serve_kernel(first, last, *refs):
    refs = list(refs)
    box_ref, power_ref = refs[:2]
    if first:
        power_out, low_out, rate_out, inv_out, gain_ref, average_ref, cell_ref = refs[2:]
    elif last:
        gain_ref, average_ref, cell_ref, power_out, return_out, rate_out = refs[2:]
    else:
        gain_ref, average_ref, cell_ref, power_out, low_out, rate_out, inv_out = refs[2:]
    even_core = lax.axis_index("core") == 0

    def swapped(value):
        top, bottom = value[0:16], value[16:32]
        return jnp.concatenate(
            [jnp.where(even_core, top, bottom), jnp.where(even_core, bottom, top)], axis=0
        )

    power = power_ref[...]
    power_here = swapped(power)
    cells_down = lax.broadcasted_iota(jnp.int32, (BLK, BLK), 0)
    low = half_mask(16)

    def one_pair(pair):
        even = box_ref[2 * pair].astype(F32)
        odd = box_ref[2 * pair + 1].astype(F32)
        upper = jnp.where(low, even[0:16], pltpu.roll(odd[0:16], CAP, axis=1))
        lower = jnp.where(low, pltpu.roll(even[0:16], CAP, axis=1), odd[0:16])
        if first:
            packed = from_spare(even, 0) + from_spare(odd, CAP)
            gain = packed[0:1] + packed[1:2] + packed[2:3]
            average = packed[3:4] + packed[4:5] + packed[5:6]
            average = jnp.where(gain > 0.0, average, 1.0)
            cell = packed[6:7].astype(jnp.int32)
            gain_ref[pl.ds(pair, 1), :] = gain
            average_ref[pl.ds(pair, 1), :] = average
            cell_ref[pl.ds(pair, 1), :] = cell
        else:
            gain = gain_ref[pl.ds(pair, 1), :]
            average = average_ref[pl.ds(pair, 1), :]
            cell = cell_ref[pl.ds(pair, 1), :]
        levels = jnp.concatenate([upper, lower], axis=0)
        if first:
            levels = jnp.where(gain > 0.0, levels, 0.0)
        index = wide(cell)
        serving = jnp.concatenate(
            [take_lanes(power_here[8 * g : 8 * g + 8], index) for g in range(4)], axis=0
        )
        rate = jnp.log1p(gain * serving / (levels + NOISE_FLOOR))
        rate_out[pair] = rate
        metric = rate * (1.0 / average)
        high = metric.astype(BF16)
        rest = (metric - high.astype(F32)).astype(BF16)
        onehot = (cells_down == cell).astype(BF16)
        return jnp.concatenate([high, rest], axis=0), onehot

    def step(i, total):
        pieces = [one_pair(8 * i + k) for k in range(8)]
        metric = jnp.concatenate([piece[0] for piece in pieces], axis=1)
        onehot = jnp.concatenate([piece[1] for piece in pieces], axis=1)
        return total + lax.dot_general(
            metric, onehot, (((1,), (1,)), ((), ())), preferred_element_type=F32
        )

    total = lax.fori_loop(0, PAIRS // 8, step, jnp.zeros((2 * SUB, BLK), F32))
    load_here = total[0:SUB] + total[SUB : 2 * SUB]
    inv = jnp.where(load_here > 0.0, 1.0 / load_here, 0.0)
    demand = 1.0 + swapped(load_here)
    new_power = 0.5 * power + 0.5 * SUB * demand / jnp.sum(demand, axis=0, keepdims=True)
    power_out[...] = new_power
    if not last:
        fresh = new_power.astype(BF16)
        for k in range(UE_COUNT):
            low_out[k] = fresh
        inv_out[...] = inv
        return

    def finish(i, carry):
        for k in range(8):
            pair = 8 * i + k
            gain = gain_ref[pl.ds(pair, 1), :]
            average = average_ref[pl.ds(pair, 1), :]
            cell = cell_ref[pl.ds(pair, 1), :]
            new = new_average(rate_out[pair], inv, gain, average, cell)
            return_out[2 * pair] = new
            return_out[2 * pair + 1] = new
        return carry

    lax.fori_loop(0, PAIRS // 8, finish, 0)


def serve(box, power, records=None, last=False):
    first = records is None
    operands = [box, power] + ([] if first else list(records))
    shapes = [jax.ShapeDtypeStruct((SUB, BLK), F32)]
    rates = (PAIRS, SUB, BLK)
    if last:
        shapes += [jax.ShapeDtypeStruct((DEVICES, 1, BLK), F32)]
    else:
        shapes += [
            jax.ShapeDtypeStruct((UE_COUNT, SUB, BLK), BF16),
            jax.ShapeDtypeStruct(rates, F32),
            jax.ShapeDtypeStruct((SUB, BLK), F32),
        ]
    if first:
        shapes += [
            jax.ShapeDtypeStruct((PAIRS, BLK), F32),
            jax.ShapeDtypeStruct((PAIRS, BLK), F32),
            jax.ShapeDtypeStruct((PAIRS, BLK), jnp.int32),
        ]
    return pl.pallas_call(
        functools.partial(serve_kernel, first, last),
        in_specs=[vmem()] * len(operands),
        out_specs=[vmem()] * len(shapes),
        out_shape=shapes,
        scratch_shapes=[pltpu.VMEM(rates, F32)] if last else [],
        compiler_params=pltpu.CompilerParams(vmem_limit_bytes=8 << 20),
        cost_estimate=pl.CostEstimate(
            flops=1 << 27, bytes_accessed=2 << 20, transcendentals=1 << 18
        ),
    )(*operands)


def average_kernel(rate_ref, inv_ref, gain_ref, average_ref, cell_ref, out_ref):
    inv = inv_ref[...]

    def step(i, carry):
        for k in range(8):
            pair = 8 * i + k
            gain = gain_ref[pl.ds(pair, 1), :]
            average = average_ref[pl.ds(pair, 1), :]
            cell = cell_ref[pl.ds(pair, 1), :]
            out_ref[pl.ds(pair, 1), :] = new_average(rate_ref[pair], inv, gain, average, cell)
        return carry

    lax.fori_loop(0, PAIRS // 8, step, 0)


def update_average(rate, inv, gain, average, cell):
    return pl.pallas_call(
        average_kernel,
        in_specs=[vmem()] * 5,
        out_specs=vmem(),
        out_shape=jax.ShapeDtypeStruct((PAIRS, BLK), F32),
        compiler_params=pltpu.CompilerParams(vmem_limit_bytes=4 << 20),
        cost_estimate=pl.CostEstimate(flops=1 << 22, bytes_accessed=1 << 20, transcendentals=0),
    )(rate, inv, gain, average, cell)


def exchange(values, axis):
    return lax.all_to_all(values, axis, split_axis=0, concat_axis=0, tiled=True)


def swap_cores(values):
    return lax.ppermute(values, "core", [(0, 1), (1, 0)])


def join(own, arrived):
    return [(own[i] + arrived[i].astype(F32)).astype(BF16) for i in range(own.shape[0])]


def on_device(gains, near_blocks, serve_block, serve_cell, serve_gain, power_init, avg_init):
    everyone = ("ue", "x", "core")
    table = exchange(copies(power_init), "ue")
    near = near_blocks.T.reshape(-1)
    destination = serve_block[:, 0]
    rows = destination.shape[0]
    matches = destination[:, None] == jnp.arange(DEVICES, dtype=jnp.int32)[None, :]
    counts = jnp.cumsum(matches.astype(jnp.int32), axis=0)
    position = jnp.sum(jnp.where(matches, counts, 0), axis=1) - 1
    number = jnp.arange(rows, dtype=jnp.int32)
    totals = counts[-1]
    offsets = jnp.cumsum(totals) - totals
    place = position + jnp.sum(jnp.where(matches, offsets[None, :], 0), axis=1)
    lanes = jnp.arange(BLK, dtype=jnp.int32)
    place_lane = (place % BLK)[:, None] == lanes[None, :]
    located = jnp.concatenate(
        [
            jnp.where(place_lane, (number % BLK)[:, None], 0),
            jnp.where(place_lane, (number // BLK)[:, None], 0),
        ],
        axis=1,
    ).astype(BF16)
    place_row = (place // BLK)[:, None] == jnp.arange(CHUNK, dtype=jnp.int32)[None, :]
    found = lax.dot_general(
        place_row.astype(BF16), located, (((0,), (0,)), ((), ())), preferred_element_type=F32
    ).astype(jnp.int32)
    order_lane, order_blk = found[:, :BLK], found[:, BLK:]
    start = jnp.minimum(offsets.reshape(PAIRS, 2)[:, 0] // BLK, CHUNK - 1)
    slot = jnp.arange(CAP, dtype=jnp.int32)
    source = (
        offsets.reshape(PAIRS, 2, 1) + slot[None, None, :] - (start * BLK)[:, None, None]
    )
    filled = slot[None, None, :] < totals.reshape(PAIRS, 2, 1)
    slot_lane = (source % BLK).reshape(PAIRS, BLK)
    slot_part = jnp.where(filled, source // BLK, 2).reshape(PAIRS, BLK)
    routing = (start, order_lane, order_blk, slot_lane, slot_part)

    home = tuple(
        value.reshape(CHUNK, BLK) for value in (serve_gain, avg_init, serve_cell)
    )

    table, near, routing, home = lax.optimization_barrier((table, near, routing, home))
    power = power_init
    for slot in range(SLOTS):
        if slot == 0:
            away, kept_sibling = first_levels(False, near, table, gains, BF16)
            mine, kept_own = first_levels(True, near, table, gains, F32)
            summed = join(mine, swap_cores(away))
        else:
            away = partial_levels(False, SPLIT, near, table, kept_sibling, BF16)
            arrived = [swap_cores(values) for values in away]
            table, _ = lax.optimization_barrier((table, away))
            summed = []
            for chunks, values in zip(SPLIT, arrived):
                (mine,) = partial_levels(True, (chunks,), near, table, kept_own, F32)
                summed += join(mine, values)
                table, summed[-1] = lax.optimization_barrier((table, summed[-1]))
        parts = [
            lax.ppermute(value, "x", [(i, (i + hop) % X_COUNT) for i in range(X_COUNT)])
            for value, hop in zip(summed[:3], HOPS)
        ]
        here = summed[3]
        if slot > 0:
            rate, here = lax.optimization_barrier((rate, here))
            average = update_average(rate, inv, gain, average, cell)
            here, average = lax.optimization_barrier((here, average))
        box = exchange(route([here] + parts, *routing, home if slot == 0 else None), everyone)
        if slot == 0:
            power, low, rate, inv, gain, average, cell = serve(box, power)
        elif slot < SLOTS - 1:
            power, low, rate, inv = serve(box, power, (gain, average, cell))
        else:
            power, leaving = serve(box, power, (gain, average, cell), True)
        if slot < SLOTS - 1:
            table = exchange(low, "ue")
    returned = exchange(leaving, everyone)[:, 0]
    returned = jnp.where(lax.axis_index("core") == 0, returned[:, :CAP], returned[:, CAP:])
    picked = lax.dot_general(
        returned,
        matches.astype(F32),
        (((0,), (1,)), ((), ())),
        precision=lax.Precision.HIGHEST,
        preferred_element_type=F32,
    )
    average_home = jnp.sum(
        jnp.where(position[None, :] == jnp.arange(CAP, dtype=jnp.int32)[:, None], picked, 0.0), axis=0
    )
    return (average_home, power)


def solution(mesh):
    inner = Mesh(mesh.devices.reshape(UE_COUNT, X_COUNT, 2), ("ue", "x", "core"))
    cell = ("x", "core")
    every = ("ue", "x", "core")
    return jax.shard_map(
        on_device,
        mesh=inner,
        in_specs=(
            P("ue", cell, None, None),
            P("ue", cell),
            P(every, None),
            P(every),
            P(every),
            P(None, every),
            P(every),
        ),
        out_specs=(P(every), P(None, every)),
        check_vma=False,
    )
```

```python
import functools
import jax
import jax.numpy as jnp
from jax import lax
from jax.experimental import pallas as pl
from jax.experimental.pallas import tpu as pltpu
from jax.sharding import Mesh, PartitionSpec as P

SLOTS = 4
NOISE_FLOOR = 0.5
KEEP_RATE = 0.7
NEW_RATE = 0.3
SUB = 32
BLK = 128
CAP = 64
FILLED = 48
DEVICES = 128
PAIRS = DEVICES // 2
CHUNK = 16
HALF = 8
BLOCKS = 128
SPLIT = ((0,), (1, 2, 3))
UE_COUNT = 16
X_COUNT = 4
HOPS = (2, 1, 3, 0)
BF16 = jnp.bfloat16
F32 = jnp.float32


def vmem():
    return pl.BlockSpec(memory_space=pltpu.VMEM)


def take_lanes(values, index):
    return jnp.take_along_axis(values, index, axis=1, mode="promise_in_bounds")


def block_levels(near, table_ref, block, weights):
    chosen = jnp.concatenate([table_ref[near[k * BLOCKS + block] >> 3] for k in range(4)], axis=1)
    return jnp.dot(chosen, weights.reshape(4 * BLK, BLK), preferred_element_type=F32)


def product_cost(blocks):
    return pl.CostEstimate(
        flops=blocks * 2 * SUB * 4 * BLK * BLK,
        bytes_accessed=blocks * 4 * BLK * BLK * 2,
        transcendentals=0,
    )


def block_order(own):
    core = lax.axis_index("core")
    core = core if own else 1 - core
    return [2 * ((lax.axis_index("x") + hop) % X_COUNT) + core for hop in HOPS]


def first_kernel(own, near, table_ref, gains_ref, out_ref, kept_ref, sems):
    order = block_order(own)

    def piece(step):
        chunk, half = step // 2, step % 2
        source = gains_ref.at[pl.ds(order[chunk] * CHUNK + half * HALF, HALF)]
        return pltpu.make_async_copy(
            source, kept_ref.at[chunk, half * HALF : half * HALF + HALF], sems.at[step]
        )

    pieces = [piece(step) for step in range(2 * X_COUNT)]
    for copy in pieces:
        copy.start()
    for step in range(2 * X_COUNT):
        chunk, half = step // 2, step % 2
        pieces[step].wait()
        for row in range(half * HALF, half * HALF + HALF):
            out_ref[chunk, row] = block_levels(
                near, table_ref, order[chunk] * CHUNK + row, kept_ref[chunk, row]
            ).astype(out_ref.dtype)


def first_levels(own, near, table, gains, dtype):
    smem = pl.BlockSpec(memory_space=pltpu.SMEM)
    return pl.pallas_call(
        functools.partial(first_kernel, own),
        in_specs=[smem, vmem(), pl.BlockSpec(memory_space=pltpu.HBM)],
        out_specs=[vmem(), vmem()],
        out_shape=[
            jax.ShapeDtypeStruct((X_COUNT, CHUNK, SUB, BLK), dtype),
            jax.ShapeDtypeStruct((X_COUNT, CHUNK, 4, BLK, BLK), BF16),
        ],
        scratch_shapes=[pltpu.SemaphoreType.DMA((2 * X_COUNT,))],
        compiler_params=pltpu.CompilerParams(vmem_limit_bytes=20 << 20),
        cost_estimate=product_cost(X_COUNT * CHUNK),
    )(near, table, pltpu.with_memory_space_constraint(gains, pltpu.HBM))


def dot_kernel(own, groups, near, table_ref, kept_ref, *out_refs):
    order = block_order(own)
    for chunks, out_ref in zip(groups, out_refs):
        for place, chunk in enumerate(chunks):
            for row in range(CHUNK):
                out_ref[place, row] = block_levels(
                    near, table_ref, order[chunk] * CHUNK + row, kept_ref[chunk, row]
                ).astype(out_ref.dtype)


def partial_levels(own, groups, near, table, kept, dtype):
    smem = pl.BlockSpec(memory_space=pltpu.SMEM)
    return pl.pallas_call(
        functools.partial(dot_kernel, own, groups),
        in_specs=[smem, vmem(), vmem()],
        out_specs=[vmem() for _ in groups],
        out_shape=[
            jax.ShapeDtypeStruct((len(chunks), CHUNK, SUB, BLK), dtype) for chunks in groups
        ],
        compiler_params=pltpu.CompilerParams(vmem_limit_bytes=12 << 20),
        cost_estimate=pl.CostEstimate(flops=1 << 10, bytes_accessed=1 << 10, transcendentals=0),
    )(near, table, kept)


def copies_kernel(power_ref, out_ref):
    low = power_ref[...].astype(BF16)
    for k in range(UE_COUNT):
        out_ref[k] = low


def copies(power):
    return pl.pallas_call(
        copies_kernel,
        in_specs=[vmem()],
        out_specs=vmem(),
        out_shape=jax.ShapeDtypeStruct((UE_COUNT, SUB, BLK), BF16),
    )(power)


def half_mask(rows):
    return lax.broadcasted_iota(jnp.int32, (rows, BLK), 1) < CAP


def three_parts(value):
    high = value.astype(BF16).astype(F32)
    middle = (value - high).astype(BF16).astype(F32)
    return high, middle, value - high - middle


def wide(row):
    return jnp.broadcast_to(row, (8, BLK))


def lanes_of(rows):
    return lax.broadcasted_iota(jnp.int32, (rows, BLK), 1)


def with_spare(chunk, packed, base):
    turned = [pltpu.roll(packed, (shift - base) % BLK, axis=1) for shift in (48, 32, 80)]
    lane = lanes_of(16) % CAP
    spare = jnp.where(
        lanes_of(16) < CAP,
        jnp.concatenate(turned[0:2], axis=0),
        jnp.concatenate([turned[2], jnp.zeros((8, BLK), F32)], axis=0),
    )
    return jnp.where(lane >= FILLED, spare, chunk)


def from_spare(chunk, base):
    lane = lanes_of(8) - base
    first = pltpu.roll(chunk[0:8], (80 + base) % BLK, axis=1)
    second = pltpu.roll(chunk[8:16], (96 + base) % BLK, axis=1)
    third = pltpu.roll(chunk[0:8], (48 + base) % BLK, axis=1)
    packed = jnp.where(lane < 16, first, jnp.where(lane < 32, second, third))
    return jnp.where((lane >= 0) & (lane < FILLED), packed, 0.0)


def route_kernel(with_records, start, *refs):
    if with_records:
        own, r1, r2, r3, order_lane, order_blk, slot_lane, slot_part, gains, averages, cells, out_ref, levels, ordered = refs
    else:
        own, r1, r2, r3, order_lane, order_blk, slot_lane, slot_part, out_ref, levels, ordered = refs
    groups = 5 if with_records else 4
    levels[:, 0:SUB] = (own[...].astype(F32) + r1[...].astype(F32)) + (
        r2[...].astype(F32) + r3[...].astype(F32)
    )
    if with_records:
        records = list(three_parts(gains[...])) + list(three_parts(averages[...]))
        records += [cells[...].astype(F32), jnp.zeros((CHUNK, BLK), F32)]
        for place, record in enumerate(records):
            levels[:, SUB + place] = record
    ordered[CHUNK] = jnp.zeros_like(ordered[CHUNK])

    for j in range(CHUNK):
        lane = wide(order_lane[j : j + 1, :])
        blk = wide(order_blk[j : j + 1, :])
        rows = [jnp.zeros((8, BLK), F32) for _ in range(groups)]
        for k in range(CHUNK):
            hit = blk == k
            for g in range(groups):
                rows[g] = jnp.where(hit, take_lanes(levels[k, 8 * g : 8 * g + 8], lane), rows[g])
        for g in range(groups):
            ordered[j, 8 * g : 8 * g + 8] = rows[g]

    def one_pair(pair):
        first = start[pair]
        lane = wide(slot_lane[pl.ds(pair, 1), :])
        part = wide(slot_part[pl.ds(pair, 1), :])
        lane_turned = pltpu.roll(lane, CAP, axis=1)
        part_turned = pltpu.roll(part, CAP, axis=1)

        def fetch(g, lane, part):
            near = take_lanes(ordered[first, 8 * g : 8 * g + 8], lane)
            far = take_lanes(ordered[first + 1, 8 * g : 8 * g + 8], lane)
            return jnp.where(part == 0, near, jnp.where(part == 1, far, 0.0))

        upper = jnp.concatenate([fetch(0, lane, part), fetch(1, lane, part)], axis=0)
        lower = jnp.concatenate(
            [fetch(2, lane_turned, part_turned), fetch(3, lane_turned, part_turned)], axis=0
        )
        low = half_mask(16)
        even = jnp.where(low, upper, lower)
        odd = jnp.where(low, lower, upper)
        if with_records:
            packed = fetch(4, lane, part)
            even = with_spare(even, packed, 0)
            odd = with_spare(odd, packed, CAP)
        out_ref[2 * pair] = even.astype(BF16)
        out_ref[2 * pair + 1] = odd.astype(BF16)

    def slot_step(i, carry):
        for k in range(8):
            one_pair(8 * i + k)
        return carry

    lax.fori_loop(0, PAIRS // 8, slot_step, 0)


def route(parts, start, order_lane, order_blk, slot_lane, slot_part, records=None):
    with_records = records is not None
    rows = SUB + 8 if with_records else SUB
    operands = list(parts) + [order_lane, order_blk, slot_lane, slot_part]
    operands += list(records) if with_records else []
    return pl.pallas_call(
        functools.partial(route_kernel, with_records),
        in_specs=[pl.BlockSpec(memory_space=pltpu.SMEM)] + [vmem()] * len(operands),
        out_specs=vmem(),
        out_shape=jax.ShapeDtypeStruct((DEVICES, 16, BLK), BF16),
        scratch_shapes=[
            pltpu.VMEM((CHUNK, rows, BLK), F32),
            pltpu.VMEM((CHUNK + 1, rows, BLK), F32),
        ],
        compiler_params=pltpu.CompilerParams(vmem_limit_bytes=6 << 20),
        cost_estimate=pl.CostEstimate(flops=8 << 20, bytes_accessed=1 << 20, transcendentals=0),
    )(start, *operands)


def new_average(rate, inv, gain, average, cell):
    index = wide(cell)
    spread = jnp.concatenate(
        [take_lanes(inv[8 * g : 8 * g + 8], index) for g in range(4)], axis=0
    )
    served = jnp.sum(rate * rate * spread, axis=0, keepdims=True) / average
    return jnp.where(gain > 0.0, KEEP_RATE * average + NEW_RATE * served, 1.0)


def serve_kernel(first, last, *refs):
    refs = list(refs)
    box_ref, power_ref = refs[:2]
    if first:
        power_out, low_out, rate_out, inv_out, gain_ref, average_ref, cell_ref = refs[2:]
    elif last:
        gain_ref, average_ref, cell_ref, power_out, return_out, rate_out = refs[2:]
    else:
        gain_ref, average_ref, cell_ref, power_out, low_out, rate_out, inv_out = refs[2:]
    even_core = lax.axis_index("core") == 0

    def swapped(value):
        top, bottom = value[0:16], value[16:32]
        return jnp.concatenate(
            [jnp.where(even_core, top, bottom), jnp.where(even_core, bottom, top)], axis=0
        )

    power = power_ref[...]
    power_here = swapped(power)
    cells_down = lax.broadcasted_iota(jnp.int32, (BLK, BLK), 0)
    low = half_mask(16)

    def one_pair(pair):
        even = box_ref[2 * pair].astype(F32)
        odd = box_ref[2 * pair + 1].astype(F32)
        upper = jnp.where(low, even[0:16], pltpu.roll(odd[0:16], CAP, axis=1))
        lower = jnp.where(low, pltpu.roll(even[0:16], CAP, axis=1), odd[0:16])
        if first:
            packed = from_spare(even, 0) + from_spare(odd, CAP)
            gain = packed[0:1] + packed[1:2] + packed[2:3]
            average = packed[3:4] + packed[4:5] + packed[5:6]
            average = jnp.where(gain > 0.0, average, 1.0)
            cell = packed[6:7].astype(jnp.int32)
            gain_ref[pl.ds(pair, 1), :] = gain
            average_ref[pl.ds(pair, 1), :] = average
            cell_ref[pl.ds(pair, 1), :] = cell
        else:
            gain = gain_ref[pl.ds(pair, 1), :]
            average = average_ref[pl.ds(pair, 1), :]
            cell = cell_ref[pl.ds(pair, 1), :]
        levels = jnp.concatenate([upper, lower], axis=0)
        if first:
            levels = jnp.where(gain > 0.0, levels, 0.0)
        index = wide(cell)
        serving = jnp.concatenate(
            [take_lanes(power_here[8 * g : 8 * g + 8], index) for g in range(4)], axis=0
        )
        rate = jnp.log1p(gain * serving / (levels + NOISE_FLOOR))
        rate_out[pair] = rate
        metric = rate * (1.0 / average)
        high = metric.astype(BF16)
        rest = (metric - high.astype(F32)).astype(BF16)
        onehot = (cells_down == cell).astype(BF16)
        return jnp.concatenate([high, rest], axis=0), onehot

    def step(i, total):
        pieces = [one_pair(32 * i + k) for k in range(32)]
        metric = jnp.concatenate([piece[0] for piece in pieces], axis=1)
        onehot = jnp.concatenate([piece[1] for piece in pieces], axis=1)
        return total + lax.dot_general(
            metric, onehot, (((1,), (1,)), ((), ())), preferred_element_type=F32
        )

    total = lax.fori_loop(0, PAIRS // 32, step, jnp.zeros((2 * SUB, BLK), F32))
    load_here = total[0:SUB] + total[SUB : 2 * SUB]
    inv = jnp.where(load_here > 0.0, 1.0 / load_here, 0.0)
    demand = 1.0 + swapped(load_here)
    new_power = 0.5 * power + 0.5 * SUB * demand / jnp.sum(demand, axis=0, keepdims=True)
    power_out[...] = new_power
    if not last:
        fresh = new_power.astype(BF16)
        for k in range(UE_COUNT):
            low_out[k] = fresh
        inv_out[...] = inv
        return

    def finish(i, carry):
        for k in range(16):
            pair = 16 * i + k
            gain = gain_ref[pl.ds(pair, 1), :]
            average = average_ref[pl.ds(pair, 1), :]
            cell = cell_ref[pl.ds(pair, 1), :]
            new = new_average(rate_out[pair], inv, gain, average, cell)
            return_out[pl.ds(2 * pair, 2), :] = jnp.broadcast_to(new, (2, BLK))
        return carry

    lax.fori_loop(0, PAIRS // 16, finish, 0)


def serve(box, power, records=None, last=False):
    first = records is None
    operands = [box, power] + ([] if first else list(records))
    shapes = [jax.ShapeDtypeStruct((SUB, BLK), F32)]
    rates = (PAIRS, SUB, BLK)
    if last:
        shapes += [jax.ShapeDtypeStruct((DEVICES, BLK), F32)]
    else:
        shapes += [
            jax.ShapeDtypeStruct((UE_COUNT, SUB, BLK), BF16),
            jax.ShapeDtypeStruct(rates, F32),
            jax.ShapeDtypeStruct((SUB, BLK), F32),
        ]
    if first:
        shapes += [
            jax.ShapeDtypeStruct((PAIRS, BLK), F32),
            jax.ShapeDtypeStruct((PAIRS, BLK), F32),
            jax.ShapeDtypeStruct((PAIRS, BLK), jnp.int32),
        ]
    return pl.pallas_call(
        functools.partial(serve_kernel, first, last),
        in_specs=[vmem()] * len(operands),
        out_specs=[vmem()] * len(shapes),
        out_shape=shapes,
        scratch_shapes=[pltpu.VMEM(rates, F32)] if last else [],
        compiler_params=pltpu.CompilerParams(vmem_limit_bytes=8 << 20),
        cost_estimate=pl.CostEstimate(
            flops=1 << 27, bytes_accessed=2 << 20, transcendentals=1 << 18
        ),
    )(*operands)


def average_kernel(rate_ref, inv_ref, gain_ref, average_ref, cell_ref, out_ref):
    inv = inv_ref[...]

    def step(i, carry):
        for k in range(8):
            pair = 8 * i + k
            gain = gain_ref[pl.ds(pair, 1), :]
            average = average_ref[pl.ds(pair, 1), :]
            cell = cell_ref[pl.ds(pair, 1), :]
            out_ref[pl.ds(pair, 1), :] = new_average(rate_ref[pair], inv, gain, average, cell)
        return carry

    lax.fori_loop(0, PAIRS // 8, step, 0)


def update_average(rate, inv, gain, average, cell):
    return pl.pallas_call(
        average_kernel,
        in_specs=[vmem()] * 5,
        out_specs=vmem(),
        out_shape=jax.ShapeDtypeStruct((PAIRS, BLK), F32),
        compiler_params=pltpu.CompilerParams(vmem_limit_bytes=4 << 20),
        cost_estimate=pl.CostEstimate(flops=1 << 22, bytes_accessed=1 << 20, transcendentals=0),
    )(rate, inv, gain, average, cell)


def exchange(values, axis):
    return lax.all_to_all(values, axis, split_axis=0, concat_axis=0, tiled=True)


def swap_cores(values):
    return lax.ppermute(values, "core", [(0, 1), (1, 0)])


def join(own, arrived):
    return [(own[i] + arrived[i].astype(F32)).astype(BF16) for i in range(own.shape[0])]


def on_device(gains, near_blocks, serve_block, serve_cell, serve_gain, power_init, avg_init):
    everyone = ("ue", "x", "core")
    table = exchange(copies(power_init), "ue")
    near = near_blocks.T.reshape(-1)
    destination = serve_block[:, 0]
    rows = destination.shape[0]
    matches = destination[:, None] == jnp.arange(DEVICES, dtype=jnp.int32)[None, :]
    counts = jnp.cumsum(matches.astype(jnp.int32), axis=0)
    position = jnp.sum(jnp.where(matches, counts, 0), axis=1) - 1
    number = jnp.arange(rows, dtype=jnp.int32)
    totals = counts[-1]
    offsets = jnp.cumsum(totals) - totals
    place = position + jnp.sum(jnp.where(matches, offsets[None, :], 0), axis=1)
    lanes = jnp.arange(BLK, dtype=jnp.int32)
    place_lane = (place % BLK)[:, None] == lanes[None, :]
    located = jnp.concatenate(
        [
            jnp.where(place_lane, (number % BLK)[:, None], 0),
            jnp.where(place_lane, (number // BLK)[:, None], 0),
        ],
        axis=1,
    ).astype(BF16)
    place_row = (place // BLK)[:, None] == jnp.arange(CHUNK, dtype=jnp.int32)[None, :]
    found = lax.dot_general(
        place_row.astype(BF16), located, (((0,), (0,)), ((), ())), preferred_element_type=F32
    ).astype(jnp.int32)
    order_lane, order_blk = found[:, :BLK], found[:, BLK:]
    start = jnp.minimum(offsets.reshape(PAIRS, 2)[:, 0] // BLK, CHUNK - 1)
    slot = jnp.arange(CAP, dtype=jnp.int32)
    source = (
        offsets.reshape(PAIRS, 2, 1) + slot[None, None, :] - (start * BLK)[:, None, None]
    )
    filled = slot[None, None, :] < totals.reshape(PAIRS, 2, 1)
    slot_lane = (source % BLK).reshape(PAIRS, BLK)
    slot_part = jnp.where(filled, source // BLK, 2).reshape(PAIRS, BLK)
    routing = (start, order_lane, order_blk, slot_lane, slot_part)

    home = tuple(
        value.reshape(CHUNK, BLK) for value in (serve_gain, avg_init, serve_cell)
    )

    table, near, routing, home = lax.optimization_barrier((table, near, routing, home))
    power = power_init
    for slot in range(SLOTS):
        if slot == 0:
            away, kept_sibling = first_levels(False, near, table, gains, BF16)
            mine, kept_own = first_levels(True, near, table, gains, F32)
            summed = join(mine, swap_cores(away))
        else:
            away = partial_levels(False, SPLIT, near, table, kept_sibling, BF16)
            arrived = [swap_cores(values) for values in away]
            table, _ = lax.optimization_barrier((table, away))
            summed = []
            for chunks, values in zip(SPLIT, arrived):
                (mine,) = partial_levels(True, (chunks,), near, table, kept_own, F32)
                summed += join(mine, values)
                table, summed[-1] = lax.optimization_barrier((table, summed[-1]))
        parts = [
            lax.ppermute(value, "x", [(i, (i + hop) % X_COUNT) for i in range(X_COUNT)])
            for value, hop in zip(summed[:3], HOPS)
        ]
        here = summed[3]
        if slot > 0:
            rate, here = lax.optimization_barrier((rate, here))
            average = update_average(rate, inv, gain, average, cell)
            here, average = lax.optimization_barrier((here, average))
        box = exchange(route([here] + parts, *routing, home if slot == 0 else None), everyone)
        if slot == 0:
            power, low, rate, inv, gain, average, cell = serve(box, power)
        elif slot < SLOTS - 1:
            power, low, rate, inv = serve(box, power, (gain, average, cell))
        else:
            power, leaving = serve(box, power, (gain, average, cell), True)
        if slot < SLOTS - 1:
            table = exchange(low, "ue")
    returned = exchange(leaving.reshape(DEVICES, 1, BLK), everyone).reshape(DEVICES, BLK)
    returned = jnp.where(lax.axis_index("core") == 0, returned[:, :CAP], returned[:, CAP:])
    picked = lax.dot_general(
        returned,
        matches.astype(F32),
        (((0,), (1,)), ((), ())),
        precision=lax.Precision.HIGHEST,
        preferred_element_type=F32,
    )
    average_home = jnp.sum(
        jnp.where(position[None, :] == jnp.arange(CAP, dtype=jnp.int32)[:, None], picked, 0.0), axis=0
    )
    return (average_home, power)


def solution(mesh):
    inner = Mesh(mesh.devices.reshape(UE_COUNT, X_COUNT, 2), ("ue", "x", "core"))
    cell = ("x", "core")
    every = ("ue", "x", "core")
    return jax.shard_map(
        on_device,
        mesh=inner,
        in_specs=(
            P("ue", cell, None, None),
            P("ue", cell),
            P(every, None),
            P(every),
            P(every),
            P(None, every),
            P(every),
        ),
        out_specs=(P(every), P(None, every)),
        check_vma=False,
    )
```

```python
import functools
import jax
import jax.numpy as jnp
from jax import lax
from jax.experimental import pallas as pl
from jax.experimental.pallas import tpu as pltpu
from jax.sharding import Mesh, PartitionSpec as P

SLOTS = 4
NOISE_FLOOR = 0.5
KEEP_RATE = 0.7
NEW_RATE = 0.3
SUB = 32
BLK = 128
CAP = 64
FILLED = 48
DEVICES = 128
PAIRS = DEVICES // 2
CHUNK = 16
HALF = 8
BLOCKS = 128
SPLIT = ((0,), (1, 2, 3))
UE_COUNT = 16
X_COUNT = 4
BF16 = jnp.bfloat16
F32 = jnp.float32


def vmem():
    return pl.BlockSpec(memory_space=pltpu.VMEM)


def take_lanes(values, index):
    return jnp.take_along_axis(values, index, axis=1, mode="promise_in_bounds")


def block_levels(near, table_ref, block, weights):
    chosen = jnp.concatenate([table_ref[near[k * BLOCKS + block] >> 3] for k in range(4)], axis=1)
    return jnp.dot(chosen, weights.reshape(4 * BLK, BLK), preferred_element_type=F32)


def product_cost(blocks):
    return pl.CostEstimate(
        flops=blocks * 2 * SUB * 4 * BLK * BLK,
        bytes_accessed=blocks * 4 * BLK * BLK * 2,
        transcendentals=0,
    )


def block_order(own):
    core = lax.axis_index("core")
    core = core if own else 1 - core
    x = lax.axis_index("x")
    side = 2 * (x % 2)
    return [2 * ((x + hop) % X_COUNT) + core for hop in (2, 1 + side, 3 - side, 0)]


def first_kernel(own, near, table_ref, gains_ref, out_ref, kept_ref, sems):
    order = block_order(own)

    def piece(step):
        chunk, half = step // 2, step % 2
        source = gains_ref.at[pl.ds(order[chunk] * CHUNK + half * HALF, HALF)]
        return pltpu.make_async_copy(
            source, kept_ref.at[chunk, half * HALF : half * HALF + HALF], sems.at[step]
        )

    pieces = [piece(step) for step in range(2 * X_COUNT)]
    for copy in pieces:
        copy.start()
    for step in range(2 * X_COUNT):
        chunk, half = step // 2, step % 2
        pieces[step].wait()
        for row in range(half * HALF, half * HALF + HALF):
            out_ref[chunk, row] = block_levels(
                near, table_ref, order[chunk] * CHUNK + row, kept_ref[chunk, row]
            ).astype(out_ref.dtype)


def first_levels(own, near, table, gains, dtype):
    smem = pl.BlockSpec(memory_space=pltpu.SMEM)
    return pl.pallas_call(
        functools.partial(first_kernel, own),
        in_specs=[smem, vmem(), pl.BlockSpec(memory_space=pltpu.HBM)],
        out_specs=[vmem(), vmem()],
        out_shape=[
            jax.ShapeDtypeStruct((X_COUNT, CHUNK, SUB, BLK), dtype),
            jax.ShapeDtypeStruct((X_COUNT, CHUNK, 4, BLK, BLK), BF16),
        ],
        scratch_shapes=[pltpu.SemaphoreType.DMA((2 * X_COUNT,))],
        compiler_params=pltpu.CompilerParams(vmem_limit_bytes=20 << 20),
        cost_estimate=product_cost(X_COUNT * CHUNK),
    )(near, table, pltpu.with_memory_space_constraint(gains, pltpu.HBM))


def dot_kernel(own, groups, near, table_ref, kept_ref, *out_refs):
    order = block_order(own)
    for chunks, out_ref in zip(groups, out_refs):
        for place, chunk in enumerate(chunks):
            for row in range(CHUNK):
                out_ref[place, row] = block_levels(
                    near, table_ref, order[chunk] * CHUNK + row, kept_ref[chunk, row]
                ).astype(out_ref.dtype)


def partial_levels(own, groups, near, table, kept, dtype):
    smem = pl.BlockSpec(memory_space=pltpu.SMEM)
    return pl.pallas_call(
        functools.partial(dot_kernel, own, groups),
        in_specs=[smem, vmem(), vmem()],
        out_specs=[vmem() for _ in groups],
        out_shape=[
            jax.ShapeDtypeStruct((len(chunks), CHUNK, SUB, BLK), dtype) for chunks in groups
        ],
        compiler_params=pltpu.CompilerParams(vmem_limit_bytes=12 << 20),
        cost_estimate=pl.CostEstimate(flops=1 << 10, bytes_accessed=1 << 10, transcendentals=0),
    )(near, table, kept)


def copies_kernel(power_ref, out_ref):
    low = power_ref[...].astype(BF16)
    for k in range(UE_COUNT):
        out_ref[k] = low


def copies(power):
    return pl.pallas_call(
        copies_kernel,
        in_specs=[vmem()],
        out_specs=vmem(),
        out_shape=jax.ShapeDtypeStruct((UE_COUNT, SUB, BLK), BF16),
    )(power)


def half_mask(rows):
    return lax.broadcasted_iota(jnp.int32, (rows, BLK), 1) < CAP


def three_parts(value):
    high = value.astype(BF16).astype(F32)
    middle = (value - high).astype(BF16).astype(F32)
    return high, middle, value - high - middle


def wide(row):
    return jnp.broadcast_to(row, (8, BLK))


def lanes_of(rows):
    return lax.broadcasted_iota(jnp.int32, (rows, BLK), 1)


def with_spare(chunk, packed, base):
    turned = [pltpu.roll(packed, (shift - base) % BLK, axis=1) for shift in (48, 32, 80)]
    lane = lanes_of(16) % CAP
    spare = jnp.where(
        lanes_of(16) < CAP,
        jnp.concatenate(turned[0:2], axis=0),
        jnp.concatenate([turned[2], jnp.zeros((8, BLK), F32)], axis=0),
    )
    return jnp.where(lane >= FILLED, spare, chunk)


def from_spare(chunk, base):
    lane = lanes_of(8) - base
    first = pltpu.roll(chunk[0:8], (80 + base) % BLK, axis=1)
    second = pltpu.roll(chunk[8:16], (96 + base) % BLK, axis=1)
    third = pltpu.roll(chunk[0:8], (48 + base) % BLK, axis=1)
    packed = jnp.where(lane < 16, first, jnp.where(lane < 32, second, third))
    return jnp.where((lane >= 0) & (lane < FILLED), packed, 0.0)


def route_kernel(with_records, start, *refs):
    if with_records:
        own, r1, r2, r3, order_lane, order_blk, slot_lane, slot_part, gains, averages, cells, out_ref, levels, ordered = refs
    else:
        own, r1, r2, r3, order_lane, order_blk, slot_lane, slot_part, out_ref, levels, ordered = refs
    groups = 5 if with_records else 4
    levels[:, 0:SUB] = (own[...].astype(F32) + r1[...].astype(F32)) + (
        r2[...].astype(F32) + r3[...].astype(F32)
    )
    if with_records:
        records = list(three_parts(gains[...])) + list(three_parts(averages[...]))
        records += [cells[...].astype(F32), jnp.zeros((CHUNK, BLK), F32)]
        for place, record in enumerate(records):
            levels[:, SUB + place] = record
    ordered[CHUNK] = jnp.zeros_like(ordered[CHUNK])

    for j in range(CHUNK):
        lane = wide(order_lane[j : j + 1, :])
        blk = wide(order_blk[j : j + 1, :])
        rows = [jnp.zeros((8, BLK), F32) for _ in range(groups)]
        for k in range(CHUNK):
            hit = blk == k
            for g in range(groups):
                rows[g] = jnp.where(hit, take_lanes(levels[k, 8 * g : 8 * g + 8], lane), rows[g])
        for g in range(groups):
            ordered[j, 8 * g : 8 * g + 8] = rows[g]

    def one_pair(pair):
        first = start[pair]
        lane = wide(slot_lane[pl.ds(pair, 1), :])
        part = wide(slot_part[pl.ds(pair, 1), :])
        lane_turned = pltpu.roll(lane, CAP, axis=1)
        part_turned = pltpu.roll(part, CAP, axis=1)

        def fetch(g, lane, part):
            near = take_lanes(ordered[first, 8 * g : 8 * g + 8], lane)
            far = take_lanes(ordered[first + 1, 8 * g : 8 * g + 8], lane)
            return jnp.where(part == 0, near, jnp.where(part == 1, far, 0.0))

        upper = jnp.concatenate([fetch(0, lane, part), fetch(1, lane, part)], axis=0)
        lower = jnp.concatenate(
            [fetch(2, lane_turned, part_turned), fetch(3, lane_turned, part_turned)], axis=0
        )
        low = half_mask(16)
        even = jnp.where(low, upper, lower)
        odd = jnp.where(low, lower, upper)
        if with_records:
            packed = fetch(4, lane, part)
            even = with_spare(even, packed, 0)
            odd = with_spare(odd, packed, CAP)
        out_ref[2 * pair] = even.astype(BF16)
        out_ref[2 * pair + 1] = odd.astype(BF16)

    def slot_step(i, carry):
        for k in range(8):
            one_pair(8 * i + k)
        return carry

    lax.fori_loop(0, PAIRS // 8, slot_step, 0)


def route(parts, start, order_lane, order_blk, slot_lane, slot_part, records=None):
    with_records = records is not None
    rows = SUB + 8 if with_records else SUB
    operands = list(parts) + [order_lane, order_blk, slot_lane, slot_part]
    operands += list(records) if with_records else []
    return pl.pallas_call(
        functools.partial(route_kernel, with_records),
        in_specs=[pl.BlockSpec(memory_space=pltpu.SMEM)] + [vmem()] * len(operands),
        out_specs=vmem(),
        out_shape=jax.ShapeDtypeStruct((DEVICES, 16, BLK), BF16),
        scratch_shapes=[
            pltpu.VMEM((CHUNK, rows, BLK), F32),
            pltpu.VMEM((CHUNK + 1, rows, BLK), F32),
        ],
        compiler_params=pltpu.CompilerParams(vmem_limit_bytes=6 << 20),
        cost_estimate=pl.CostEstimate(flops=8 << 20, bytes_accessed=1 << 20, transcendentals=0),
    )(start, *operands)


def new_average(rate, inv, gain, average, cell):
    index = wide(cell)
    spread = jnp.concatenate(
        [take_lanes(inv[8 * g : 8 * g + 8], index) for g in range(4)], axis=0
    )
    served = jnp.sum(rate * rate * spread, axis=0, keepdims=True) / average
    return jnp.where(gain > 0.0, KEEP_RATE * average + NEW_RATE * served, 1.0)


def serve_kernel(first, last, *refs):
    refs = list(refs)
    box_ref, power_ref = refs[:2]
    if first:
        power_out, low_out, rate_out, inv_out, gain_ref, average_ref, cell_ref = refs[2:]
    elif last:
        gain_ref, average_ref, cell_ref, power_out, return_out, rate_out = refs[2:]
    else:
        gain_ref, average_ref, cell_ref, power_out, low_out, rate_out, inv_out = refs[2:]
    even_core = lax.axis_index("core") == 0

    def swapped(value):
        top, bottom = value[0:16], value[16:32]
        return jnp.concatenate(
            [jnp.where(even_core, top, bottom), jnp.where(even_core, bottom, top)], axis=0
        )

    power = power_ref[...]
    power_here = swapped(power)
    cells_down = lax.broadcasted_iota(jnp.int32, (BLK, BLK), 0)
    low = half_mask(16)

    def one_pair(pair):
        even = box_ref[2 * pair].astype(F32)
        odd = box_ref[2 * pair + 1].astype(F32)
        upper = jnp.where(low, even[0:16], pltpu.roll(odd[0:16], CAP, axis=1))
        lower = jnp.where(low, pltpu.roll(even[0:16], CAP, axis=1), odd[0:16])
        if first:
            packed = from_spare(even, 0) + from_spare(odd, CAP)
            gain = packed[0:1] + packed[1:2] + packed[2:3]
            average = packed[3:4] + packed[4:5] + packed[5:6]
            average = jnp.where(gain > 0.0, average, 1.0)
            cell = packed[6:7].astype(jnp.int32)
            gain_ref[pl.ds(pair, 1), :] = gain
            average_ref[pl.ds(pair, 1), :] = average
            cell_ref[pl.ds(pair, 1), :] = cell
        else:
            gain = gain_ref[pl.ds(pair, 1), :]
            average = average_ref[pl.ds(pair, 1), :]
            cell = cell_ref[pl.ds(pair, 1), :]
        levels = jnp.concatenate([upper, lower], axis=0)
        if first:
            levels = jnp.where(gain > 0.0, levels, 0.0)
        index = wide(cell)
        serving = jnp.concatenate(
            [take_lanes(power_here[8 * g : 8 * g + 8], index) for g in range(4)], axis=0
        )
        rate = jnp.log1p(gain * serving / (levels + NOISE_FLOOR))
        rate_out[pair] = rate
        metric = rate * (1.0 / average)
        high = metric.astype(BF16)
        rest = (metric - high.astype(F32)).astype(BF16)
        onehot = (cells_down == cell).astype(BF16)
        return jnp.concatenate([high, rest], axis=0), onehot

    def step(i, total):
        pieces = [one_pair(32 * i + k) for k in range(32)]
        metric = jnp.concatenate([piece[0] for piece in pieces], axis=1)
        onehot = jnp.concatenate([piece[1] for piece in pieces], axis=1)
        return total + lax.dot_general(
            metric, onehot, (((1,), (1,)), ((), ())), preferred_element_type=F32
        )

    total = lax.fori_loop(0, PAIRS // 32, step, jnp.zeros((2 * SUB, BLK), F32))
    load_here = total[0:SUB] + total[SUB : 2 * SUB]
    inv = jnp.where(load_here > 0.0, 1.0 / load_here, 0.0)
    demand = 1.0 + swapped(load_here)
    new_power = 0.5 * power + 0.5 * SUB * demand / jnp.sum(demand, axis=0, keepdims=True)
    power_out[...] = new_power
    if not last:
        fresh = new_power.astype(BF16)
        for k in range(UE_COUNT):
            low_out[k] = fresh
        inv_out[...] = inv
        return

    for pair in range(PAIRS):
        new = new_average(
            rate_out[pair],
            inv,
            gain_ref[pair : pair + 1, :],
            average_ref[pair : pair + 1, :],
            cell_ref[pair : pair + 1, :],
        )
        return_out[2 * pair : 2 * pair + 2, :] = jnp.broadcast_to(new, (2, BLK))


def serve(box, power, records=None, last=False):
    first = records is None
    operands = [box, power] + ([] if first else list(records))
    shapes = [jax.ShapeDtypeStruct((SUB, BLK), F32)]
    rates = (PAIRS, SUB, BLK)
    if last:
        shapes += [jax.ShapeDtypeStruct((DEVICES, BLK), F32)]
    else:
        shapes += [
            jax.ShapeDtypeStruct((UE_COUNT, SUB, BLK), BF16),
            jax.ShapeDtypeStruct(rates, F32),
            jax.ShapeDtypeStruct((SUB, BLK), F32),
        ]
    if first:
        shapes += [
            jax.ShapeDtypeStruct((PAIRS, BLK), F32),
            jax.ShapeDtypeStruct((PAIRS, BLK), F32),
            jax.ShapeDtypeStruct((PAIRS, BLK), jnp.int32),
        ]
    return pl.pallas_call(
        functools.partial(serve_kernel, first, last),
        in_specs=[vmem()] * len(operands),
        out_specs=[vmem()] * len(shapes),
        out_shape=shapes,
        scratch_shapes=[pltpu.VMEM(rates, F32)] if last else [],
        compiler_params=pltpu.CompilerParams(vmem_limit_bytes=8 << 20),
        cost_estimate=pl.CostEstimate(
            flops=1 << 27, bytes_accessed=2 << 20, transcendentals=1 << 18
        ),
    )(*operands)


def average_kernel(rate_ref, inv_ref, gain_ref, average_ref, cell_ref, out_ref):
    inv = inv_ref[...]

    def step(i, carry):
        for k in range(8):
            pair = 8 * i + k
            gain = gain_ref[pl.ds(pair, 1), :]
            average = average_ref[pl.ds(pair, 1), :]
            cell = cell_ref[pl.ds(pair, 1), :]
            out_ref[pl.ds(pair, 1), :] = new_average(rate_ref[pair], inv, gain, average, cell)
        return carry

    lax.fori_loop(0, PAIRS // 8, step, 0)


def update_average(rate, inv, gain, average, cell):
    return pl.pallas_call(
        average_kernel,
        in_specs=[vmem()] * 5,
        out_specs=vmem(),
        out_shape=jax.ShapeDtypeStruct((PAIRS, BLK), F32),
        compiler_params=pltpu.CompilerParams(vmem_limit_bytes=4 << 20),
        cost_estimate=pl.CostEstimate(flops=1 << 22, bytes_accessed=1 << 20, transcendentals=0),
    )(rate, inv, gain, average, cell)


def exchange(values, axis):
    return lax.all_to_all(values, axis, split_axis=0, concat_axis=0, tiled=True)


def swap_cores(values):
    return lax.ppermute(values, "core", [(0, 1), (1, 0)])


def trade(values, hop):
    moves = [(x, (x + (hop if x % 2 == 0 else X_COUNT - hop)) % X_COUNT) for x in range(X_COUNT)]
    return lax.ppermute(values, "x", moves)


def join(own, arrived):
    return [(own[i] + arrived[i].astype(F32)).astype(BF16) for i in range(own.shape[0])]


def on_device(gains, near_blocks, serve_block, serve_cell, serve_gain, power_init, avg_init):
    everyone = ("ue", "x", "core")
    table = exchange(copies(power_init), "ue")
    near = near_blocks.T.reshape(-1)
    destination = serve_block[:, 0]
    rows = destination.shape[0]
    matches = destination[:, None] == jnp.arange(DEVICES, dtype=jnp.int32)[None, :]
    counts = jnp.cumsum(matches.astype(jnp.int32), axis=0)
    position = jnp.sum(jnp.where(matches, counts, 0), axis=1) - 1
    number = jnp.arange(rows, dtype=jnp.int32)
    totals = counts[-1]
    offsets = jnp.cumsum(totals) - totals
    place = position + jnp.sum(jnp.where(matches, offsets[None, :], 0), axis=1)
    lanes = jnp.arange(BLK, dtype=jnp.int32)
    place_lane = (place % BLK)[:, None] == lanes[None, :]
    located = jnp.concatenate(
        [
            jnp.where(place_lane, (number % BLK)[:, None], 0),
            jnp.where(place_lane, (number // BLK)[:, None], 0),
        ],
        axis=1,
    ).astype(BF16)
    place_row = (place // BLK)[:, None] == jnp.arange(CHUNK, dtype=jnp.int32)[None, :]
    found = lax.dot_general(
        place_row.astype(BF16), located, (((0,), (0,)), ((), ())), preferred_element_type=F32
    ).astype(jnp.int32)
    order_lane, order_blk = found[:, :BLK], found[:, BLK:]
    start = jnp.minimum(offsets.reshape(PAIRS, 2)[:, 0] // BLK, CHUNK - 1)
    slot = jnp.arange(CAP, dtype=jnp.int32)
    source = (
        offsets.reshape(PAIRS, 2, 1) + slot[None, None, :] - (start * BLK)[:, None, None]
    )
    filled = slot[None, None, :] < totals.reshape(PAIRS, 2, 1)
    slot_lane = (source % BLK).reshape(PAIRS, BLK)
    slot_part = jnp.where(filled, source // BLK, 2).reshape(PAIRS, BLK)
    routing = (start, order_lane, order_blk, slot_lane, slot_part)

    home = tuple(
        value.reshape(CHUNK, BLK) for value in (serve_gain, avg_init, serve_cell)
    )

    table, near, routing, home = lax.optimization_barrier((table, near, routing, home))
    power = power_init
    for slot in range(SLOTS):
        if slot == 0:
            away, kept_sibling = first_levels(False, near, table, gains, BF16)
            mine, kept_own = first_levels(True, near, table, gains, F32)
            summed = join(mine, swap_cores(away))
        else:
            away = partial_levels(False, SPLIT, near, table, kept_sibling, BF16)
            arrived = [swap_cores(values) for values in away]
            table, _ = lax.optimization_barrier((table, away))
            summed = []
            for chunks, values in zip(SPLIT, arrived):
                (mine,) = partial_levels(True, (chunks,), near, table, kept_own, F32)
                summed += join(mine, values)
                table, summed[-1] = lax.optimization_barrier((table, summed[-1]))
        parts = [trade(value, hop) for value, hop in zip(summed[:3], (2, 1, 3))]
        here = summed[3]
        if slot > 0:
            rate, here = lax.optimization_barrier((rate, here))
            average = update_average(rate, inv, gain, average, cell)
            here, average = lax.optimization_barrier((here, average))
        box = exchange(route([here] + parts, *routing, home if slot == 0 else None), everyone)
        if slot == 0:
            power, low, rate, inv, gain, average, cell = serve(box, power)
        elif slot < SLOTS - 1:
            power, low, rate, inv = serve(box, power, (gain, average, cell))
        else:
            power, leaving = serve(box, power, (gain, average, cell), True)
        if slot < SLOTS - 1:
            table = exchange(low, "ue")
    returned = exchange(leaving.reshape(DEVICES, 1, BLK), everyone).reshape(DEVICES, BLK)
    returned = jnp.where(lax.axis_index("core") == 0, returned[:, :CAP], returned[:, CAP:])
    picked = lax.dot_general(
        returned,
        matches.astype(F32),
        (((0,), (1,)), ((), ())),
        precision=lax.Precision.HIGHEST,
        preferred_element_type=F32,
    )
    average_home = jnp.sum(
        jnp.where(position[None, :] == jnp.arange(CAP, dtype=jnp.int32)[:, None], picked, 0.0), axis=0
    )
    return (average_home, power)


def solution(mesh):
    inner = Mesh(mesh.devices.reshape(UE_COUNT, X_COUNT, 2), ("ue", "x", "core"))
    cell = ("x", "core")
    every = ("ue", "x", "core")
    return jax.shard_map(
        on_device,
        mesh=inner,
        in_specs=(
            P("ue", cell, None, None),
            P("ue", cell),
            P(every, None),
            P(every),
            P(every),
            P(None, every),
            P(every),
        ),
        out_specs=(P(every), P(None, every)),
        check_vma=False,
    )
```
